256 devices in a mesh: gx: 32 (over x, z), gy: 8 (over y, core).
Axes of the slice: x: 4, y: 4, z: 8, core: 2. Of those that a mesh axis runs over, the one named last changes fastest.
Arguments:
- flow_state: float32 [4, 512, 256, 128], P(None, 'gx', 'gy'), may hold values from -10 to 10
- viscosity: float32 [512, 256, 128], P('gx', 'gy'), may hold values from 300 to 1200
Outputs:
- flow_next: float32 [4, 512, 256, 128], P(None, 'gx', 'gy')
The draws below stay inside these ranges and needn't reach their ends.
All inputs are finite; a program needn't handle non-finite values.
Results may differ from the reference program's by a relative error of at most 0.0003.
Values sent between devices are 32-bit elements; how exact they have to be, the bound alone decides.
A program may use at most 64 MiB of HBM per device.

```python
import math
import jax
import jax.numpy as jnp
from jax import lax

FIELDS = 4
NZ = 128
STEPS = 1
NX = 512
NY = 256


def draw_flow_state(key, part):
    rough_key = jax.random.fold_in(key, 11)
    offset_key = jax.random.fold_in(key, 12)
    phase_key = jax.random.fold_in(key, 14)
    amplitude_key = jax.random.fold_in(key, 15)
    rough_part = jax.random.truncated_normal(rough_key, -3.0, 3.0, (FIELDS, NX, NY, NZ), jnp.float32)
    x_angle = jnp.arange(NX, dtype=jnp.float32).reshape(1, NX, 1, 1) * (2.0 * math.pi / NX)
    y_angle = jnp.arange(NY, dtype=jnp.float32).reshape(1, 1, NY, 1) * (2.0 * math.pi / NY)
    phases = jax.random.uniform(phase_key, (2, FIELDS, 1, 1, 1), jnp.float32, -math.pi, math.pi)
    offset = jax.random.uniform(offset_key, (FIELDS, 1, 1, 1), jnp.float32, -1.5, 1.5)
    amplitudes = jax.random.uniform(amplitude_key, (2, FIELDS, 1, 1, 1), jnp.float32, 1.5, 2.0)
    trend = amplitudes[0] * jnp.cos(x_angle + phases[0]) + amplitudes[1] * jnp.cos(y_angle + phases[1])
    return rough_part + offset + trend


def steps_of(stream_key, dims, pieces, least, high):
    factor_of = 1.0
    for dim, blocks in pieces:
        steps = jax.random.uniform(jax.random.fold_in(jax.random.fold_in(stream_key, 6), dim), (blocks,), jnp.float32, least / len(pieces), high / len(pieces))
        factor_of = factor_of * jnp.repeat(jnp.exp(steps), dims[dim] // blocks).reshape((-1,) + (1,) * (len(dims) - 1 - dim))
    return factor_of


def setup_inputs(seed: int = 0) -> dict:
    streams_of = jax.random.split(jax.random.key(seed), 3)
    flow_state = draw_flow_state(jax.random.fold_in(streams_of[2], 71), 0)
    viscosity = jnp.clip(jnp.exp(math.log(1200.0) - 1.3862944 * jax.random.uniform(streams_of[1], (NX, NY, NZ), jnp.float32) ** steps_of(streams_of[1], (NX, NY, NZ), ((0, 32), (1, 8)), -0.2, 0.2)), 300.0, 1200.0)
    return dict(flow_state=flow_state, viscosity=viscosity)


ADVECT = 0.2
BUOYANT = 0.5
CONDUCT = 0.6

def advect(flow_state):
    padded = jnp.pad(flow_state, ((0, 0), (1, 1), (1, 1), (0, 0)))
    along_x = 0.5 * (padded[:, 2:, 1:-1] - padded[:, :-2, 1:-1])
    along_y = 0.5 * (padded[:, 1:-1, 2:] - padded[:, 1:-1, :-2])
    along_z = 0.5 * (jnp.roll(flow_state, -1, 3) - jnp.roll(flow_state, 1, 3))
    carried = flow_state[0:1] * along_x + flow_state[1:2] * along_y + flow_state[2:3] * along_z
    source = flow_state - ADVECT * carried
    return jnp.concatenate([source[:2], source[2:3] + BUOYANT * flow_state[3:4], source[3:]], 0)

def solve_line(field, coefficient, along):
    moved = jnp.moveaxis(field, along, -1)
    spread = jnp.moveaxis(coefficient, along, -1)
    face_values = jnp.concatenate([spread[..., :1], 0.5 * (spread[..., :-1] + spread[..., 1:]), spread[..., -1:]], -1)
    length = moved.shape[-1]
    position = lax.broadcasted_iota(jnp.int32, moved.shape, moved.ndim - 1)
    lowers = jnp.where(position == 0, 0.0, -face_values[..., :-1])
    uppers = jnp.where(position == length - 1, 0.0, -face_values[..., 1:])
    middle = 1.0 + face_values[..., :-1] + face_values[..., 1:]
    solution = lax.linalg.tridiagonal_solve(lowers, middle, uppers, moved[..., None])[..., 0]
    return jnp.moveaxis(solution, -1, along)

def reference(flow_state, viscosity):
    coefficients = [viscosity, viscosity, viscosity, CONDUCT * viscosity]
    current = flow_state
    for repeat in range(STEPS):
        source = advect(current)
        fields = [solve_line(source[i], coefficients[i], 0) for i in range(4)]
        fields = [solve_line(fields[i], coefficients[i], 1) for i in range(4)]
        current = jnp.stack(fields)
    return current
```

```python
import functools

import jax
import jax.numpy as jnp
from jax import lax
from jax.experimental import pallas as pl
from jax.experimental.pallas import tpu as pltpu
from jax.sharding import PartitionSpec as P

MESH = pl.DeviceIdType.MESH

ADVECT = 0.2
BUOYANT = 0.5
CONDUCT = 0.6
KINDS = (1.0, CONDUCT)
KIND_OF = (0, 0, 0, 1)

NF = 4
LX, LY, NZ = 16, 32, 128
PX, PY = 32, 8
Y0 = 8


def factor(faces, along):
    inverse, lower, ratio = {}, {}, {}
    one = jnp.ones_like(faces[1])
    running = one
    forward = {}
    for k in range(1, along - 1):
        centre = 1.0 + faces[k] + faces[k + 1]
        if k > 1:
            centre = centre - faces[k] * ratio[k - 1]
        inverse[k] = 1.0 / centre
        lower[k] = faces[k] * inverse[k]
        ratio[k] = faces[k + 1] * inverse[k]
        running = lower[k] * running
        forward[k] = running
    first, last = {along - 1: jnp.zeros_like(one)}, {along - 1: one}
    for k in range(along - 2, 0, -1):
        first[k] = forward[k] + ratio[k] * first[k + 1]
        last[k] = ratio[k] * last[k + 1]
    first[0], last[0] = one, jnp.zeros_like(one)
    return inverse, lower, ratio, first, last


def keep_factor(load, along, refs, tiles):
    inv_ref, low_ref, rat_ref, first_ref, last_ref = refs
    cells = [load(k) for k in range(along)]
    middles = [None] + [cells[k - 1] + cells[k] for k in range(1, along)]
    tiles[0] = cells[0]
    tiles[1] = cells[-1]
    for kind, scale in enumerate(KINDS):
        faces = [None] + [(0.5 * scale) * m for m in middles[1:]]
        inverse, lower, ratio, first, last = factor(faces, along)
        for k in range(1, along - 1):
            inv_ref[kind, k] = inverse[k]
            low_ref[kind, k] = lower[k]
            rat_ref[kind, k] = ratio[k]
        for k in range(along):
            first_ref[kind, k] = first[k]
            last_ref[kind, k] = last[k]
        tiles[2 + kind] = 1.0 + faces[1] * (1.0 - first[1])
        tiles[4 + kind] = faces[1] * last[1]
        tiles[6 + kind] = 1.0 + faces[along - 1] * (1.0 - last[along - 2])


def rolled(value):
    return pltpu.roll(value, 4, 0)


def interface_factor(coef, base, blocks, refs):
    inv_ref, low_ref, rat_ref = refs
    sub = lax.broadcasted_iota(jnp.int32, (8, NZ), 0)
    down = sub < 4
    thermal = (sub == 3) | (sub == 7)

    def row(block, r):
        return jnp.broadcast_to(coef[pl.ds(base(block) + r, 1), :], (8, NZ))

    def by_kind(block, r):
        return jnp.where(thermal, row(block, r + 1), row(block, r))

    scale = jnp.where(thermal, CONDUCT, 1.0).astype(jnp.float32)
    half = blocks // 2
    sides = []
    for i in range(half + 1):
        if i == 0:
            value = jnp.where(down, row(0, 0), row(blocks - 1, 1))
        elif i == half:
            value = 0.5 * (row(i - 1, 1) + row(i, 0))
        else:
            value = 0.5 * jnp.where(
                down,
                row(i - 1, 1) + row(i, 0),
                row(blocks - 1 - i, 1) + row(blocks - i, 0),
            )
        sides.append(scale * value)
    ratio = None
    for i in range(half):
        j = blocks - 1 - i
        couple = jnp.where(down, by_kind(i, 4), by_kind(j, 4))
        even = jnp.where(down, by_kind(i, 2), by_kind(j, 6)) + sides[i]
        odd = jnp.where(down, by_kind(i, 6), by_kind(j, 2)) + sides[i + 1]
        for m, centre, before, after in (
            (2 * i, even, sides[i], couple),
            (2 * i + 1, odd, couple, sides[i + 1]),
        ):
            if m > 0:
                centre = centre - before * ratio
            inverse = 1.0 / centre
            ratio = after * inverse
            inv_ref[m] = inverse
            low_ref[m] = before * inverse
            rat_ref[m] = ratio
    inv_ref[blocks] = 1.0 / (1.0 - ratio * rolled(ratio))


def interface_solve(right, solved, base, blocks, refs):
    inv_ref, low_ref, rat_ref = refs
    down = lax.broadcasted_iota(jnp.int32, (8, NZ), 0) < 4
    half = blocks // 2
    forward = []
    for i in range(half):
        j = blocks - 1 - i
        mine, other = right[pl.ds(base(i), 8), :], right[pl.ds(base(j), 8), :]
        even = jnp.where(down, mine, other)
        odd = rolled(jnp.where(down, other, mine))
        for m, value in ((2 * i, even), (2 * i + 1, odd)):
            value = inv_ref[m] * value
            if m > 0:
                value = value + low_ref[m] * forward[-1]
            forward.append(value)
    tail = forward[-1]
    values = [None] * blocks
    values[-1] = (tail + rat_ref[blocks - 1] * rolled(tail)) * inv_ref[blocks]
    for m in range(blocks - 2, -1, -1):
        values[m] = forward[m] + rat_ref[m] * values[m + 1]
    for i in range(half):
        j = blocks - 1 - i
        even, odd = values[2 * i], rolled(values[2 * i + 1])
        solved[pl.ds(base(i), 8), :] = jnp.where(down, even, odd)
        solved[pl.ds(base(j), 8), :] = jnp.where(down, odd, even)


def kernel(flow, visc, out, fpad, vbuf, cur, inner, outbuf, *rest):
    xf, yf = rest[0:5], rest[5:10]
    xi, yi = rest[10:13], rest[13:19]
    yi = (yi[0:3], yi[3:6])
    cxs, cxr, cys, cyr, xs, xr, xb, xg, ys, yr, yb, yg = rest[19:31]
    in_sem, out_sem, send_sem, recv_sem, halo_send, halo_recv = rest[31:]
    gx, gy = lax.axis_index("gx"), lax.axis_index("gy")

    barrier = pltpu.get_barrier_semaphore()

    def on_x(d):
        return (lax.rem(gx + d, PX), gy)

    def on_y(d):
        return (gx, lax.rem(gy + d, PY))

    @pl.loop(1, PX)
    def _(d):
        pl.semaphore_signal(barrier, inc=1, device_id=on_x(d), device_id_type=MESH)

    @pl.loop(1, PY)
    def _(d):
        pl.semaphore_signal(barrier, inc=1, device_id=on_y(d), device_id_type=MESH)

    visc_in = pltpu.make_async_copy(visc, vbuf, in_sem.at[0])
    flow_in = pltpu.make_async_copy(
        flow, fpad.at[:, pl.ds(1, LX), pl.ds(Y0, LY), :], in_sem.at[1]
    )
    visc_in.start()
    flow_in.start()

    @pl.when(gx == 0)
    def _():
        fpad[:, 0, Y0 : Y0 + LY, :] = jnp.zeros((NF, LY, NZ), jnp.float32)

    @pl.when(gx == PX - 1)
    def _():
        fpad[:, LX + 1, Y0 : Y0 + LY, :] = jnp.zeros((NF, LY, NZ), jnp.float32)

    @pl.when(gy == 0)
    def _():
        fpad[:, 1 : LX + 1, Y0 - 1 : Y0, :] = jnp.zeros((NF, LX, 1, NZ), jnp.float32)

    @pl.when(gy == PY - 1)
    def _():
        fpad[:, 1 : LX + 1, Y0 + LY : Y0 + LY + 1, :] = jnp.zeros((NF, LX, 1, NZ), jnp.float32)

    visc_in.wait()
    tiles = {}
    keep_factor(lambda k: vbuf[pl.ds(k * LY, LY), :], LX, xf, tiles)
    for r in range(8):
        cxs[pl.ds(r, LY, stride=8), :] = tiles[r]
    tiles = {}
    keep_factor(lambda k: vbuf[pl.ds(k, LX, stride=LY), :], LY, yf, tiles)
    for r in range(8):
        cys[pl.ds(r, LX, stride=8), :] = tiles[r]

    flow_in.wait()
    pl.semaphore_wait(barrier, PX - 1 + PY - 1)

    x_low = fpad.at[:, pl.ds(0, 1), pl.ds(Y0, LY), :]
    x_first = fpad.at[:, pl.ds(1, 1), pl.ds(Y0, LY), :]
    x_last = fpad.at[:, pl.ds(LX, 1), pl.ds(Y0, LY), :]
    x_high = fpad.at[:, pl.ds(LX + 1, 1), pl.ds(Y0, LY), :]
    y_low = fpad.at[:, pl.ds(1, LX), pl.ds(Y0 - 1, 1), :]
    y_first = fpad.at[:, pl.ds(1, LX), pl.ds(Y0, 1), :]
    y_last = fpad.at[:, pl.ds(1, LX), pl.ds(Y0 + LY - 1, 1), :]
    y_high = fpad.at[:, pl.ds(1, LX), pl.ds(Y0 + LY, 1), :]

    def halo(n, src, dst, device):
        return pltpu.make_async_remote_copy(
            src_ref=src,
            dst_ref=dst,
            send_sem=halo_send.at[n],
            recv_sem=halo_recv.at[n],
            device_id=device,
            device_id_type=MESH,
        )

    x_up = halo(0, x_last, x_low, on_x(1))
    x_down = halo(1, x_first, x_high, on_x(PX - 1))
    y_up = halo(2, y_last, y_low, on_y(1))
    y_down = halo(3, y_first, y_high, on_y(PY - 1))
    has_up, has_down = gx < PX - 1, gx > 0
    has_right, has_left = gy < PY - 1, gy > 0
    pl.when(has_up)(x_up.start)
    pl.when(has_down)(x_down.start)
    pl.when(has_right)(y_up.start)
    pl.when(has_left)(y_down.start)

    def spread(src, dst, n, along_x, size):
        peers, me = (PX, gx) if along_x else (PY, gy)
        mine = pl.ds(pl.multiple_of(me * size, 8), size)

        @pl.loop(1, peers)
        def _(d):
            device = on_x(d) if along_x else on_y(d)
            there = device[0] if along_x else device[1]
            pltpu.make_async_remote_copy(
                src_ref=src.at[pl.ds(pl.multiple_of(there * size, 8), size), :],
                dst_ref=dst.at[mine, :],
                send_sem=send_sem.at[n],
                recv_sem=recv_sem.at[n],
                device_id=device,
                device_id_type=MESH,
            ).start()

        dst[mine, :] = src[mine, :]

    def arrived(dst, n, peers, size):
        part = dst.at[pl.ds(0, (peers - 1) * size), :]
        pltpu.make_async_copy(part, part, recv_sem.at[n]).wait()

    def departed(src, n, peers, size):
        part = src.at[pl.ds(0, (peers - 1) * size), :]
        pltpu.make_async_copy(part, part, send_sem.at[n]).wait()

    spread(cxs, cxr, 0, True, 8)
    spread(cys, cyr, 1, False, 16)

    pl.when(has_down)(x_up.wait_recv)
    pl.when(has_up)(x_down.wait_recv)
    pl.when(has_left)(y_up.wait_recv)
    pl.when(has_right)(y_down.wait_recv)

    _, _, _, first_ref, last_ref = xf

    def source_row(k, sums):
        here = [fpad[f, k + 1, Y0 : Y0 + LY, :] for f in range(NF)]
        done = []
        for f in range(NF):
            across_x = fpad[f, k + 2, Y0 : Y0 + LY, :] - fpad[f, k, Y0 : Y0 + LY, :]
            across_y = (
                fpad[f, k + 1, Y0 + 1 : Y0 + LY + 1, :] - fpad[f, k + 1, Y0 - 1 : Y0 + LY - 1, :]
            )
            across_z = pltpu.roll(here[f], NZ - 1, 1) - pltpu.roll(here[f], 1, 1)
            carried = here[0] * across_x + here[1] * across_y + here[2] * across_z
            source = here[f] - (0.5 * ADVECT) * carried
            if f == 2:
                source = source + BUOYANT * here[3]
            cur[f, pl.ds(pl.multiple_of(k * LY, 8), LY), :] = source
            kind = KIND_OF[f]
            done.append(sums[f] + first_ref[kind, k] * source)
            done.append(sums[NF + f] + last_ref[kind, k] * source)
        return tuple(done[0::2] + done[1::2])

    zero = jnp.zeros((LY, NZ), jnp.float32)
    sums = lax.fori_loop(0, LX, source_row, (zero,) * (2 * NF))
    for r in range(8):
        xs[pl.ds(r, LY, stride=8), :] = sums[r]
    spread(xs, xr, 2, True, 8)

    inv_ref, low_ref, rat_ref, first_ref, last_ref = xf

    def x_rows(k):
        return pl.ds(pl.multiple_of(k * LY, 8), LY)

    def x_down_row(k, before):
        result = []
        for f in range(NF):
            kind = KIND_OF[f]
            value = inv_ref[kind, k] * cur[f, x_rows(k), :] + low_ref[kind, k] * before[f]
            inner[f, x_rows(k), :] = value
            result.append(value)
        return tuple(result)

    def x_up_row(step, after):
        k = LX - 3 - step
        result = []
        for f in range(NF):
            value = inner[f, x_rows(k), :] + rat_ref[KIND_OF[f], k] * after[f]
            inner[f, x_rows(k), :] = value
            result.append(value)
        return tuple(result)

    tail = lax.fori_loop(1, LX - 1, x_down_row, (zero,) * NF)
    lax.fori_loop(0, LX - 3, x_up_row, tail)

    arrived(cxr, 0, PX, 8)
    interface_factor(cxr, lambda b: 8 * b, PX, xi)
    arrived(cyr, 1, PY, 16)
    for t in range(2):
        interface_factor(cyr, lambda b, t=t: 16 * b + 8 * t, PY, yi[t])

    arrived(xr, 2, PX, 8)
    interface_solve(xr, xb, lambda b: 8 * b, PX, xi)
    spread(xb, xg, 3, True, 8)
    arrived(xg, 3, PX, 8)

    starts = [xg[pl.ds(f, LY, stride=8), :] for f in range(NF)]
    ends = [xg[pl.ds(NF + f, LY, stride=8), :] for f in range(NF)]
    for f in range(NF):
        cur[f, pl.ds(0, LY), :] = starts[f]
        cur[f, pl.ds((LX - 1) * LY, LY), :] = ends[f]

        @pl.loop(1, LX - 1)
        def _(k, f=f):
            kind = KIND_OF[f]
            cur[f, x_rows(k), :] = (
                inner[f, x_rows(k), :]
                + first_ref[kind, k] * starts[f]
                + last_ref[kind, k] * ends[f]
            )

    inv_ref, low_ref, rat_ref, first_ref, last_ref = yf

    def y_rows(k):
        return pl.ds(k, LX, stride=LY)

    zero = jnp.zeros((LX, NZ), jnp.float32)
    sums = [zero] * (2 * NF)
    for k in range(LY):
        for f in range(NF):
            kind = KIND_OF[f]
            value = cur[f, y_rows(k), :]
            if k < LY - 1:
                sums[f] = sums[f] + first_ref[kind, k] * value
            if k > 0:
                sums[NF + f] = sums[NF + f] + last_ref[kind, k] * value
    for r in range(8):
        ys[pl.ds(r, LX, stride=8), :] = sums[r]
    spread(ys, yr, 4, False, 16)

    before = [zero] * NF
    for k in range(1, LY - 1):
        for f in range(NF):
            kind = KIND_OF[f]
            before[f] = inv_ref[kind, k] * cur[f, y_rows(k), :] + low_ref[kind, k] * before[f]
            inner[f, pl.ds(k * LX, LX), :] = before[f]
    after = before
    for k in range(LY - 3, 0, -1):
        for f in range(NF):
            after[f] = inner[f, pl.ds(k * LX, LX), :] + rat_ref[KIND_OF[f], k] * after[f]
            inner[f, pl.ds(k * LX, LX), :] = after[f]

    arrived(yr, 4, PY, 16)
    for t in range(2):
        interface_solve(yr, yb, lambda b, t=t: 16 * b + 8 * t, PY, yi[t])
    spread(yb, yg, 5, False, 16)
    arrived(yg, 5, PY, 16)

    outs = []
    for f in range(NF):
        kind = KIND_OF[f]
        start, end = yg[pl.ds(f, LX, stride=8), :], yg[pl.ds(NF + f, LX, stride=8), :]
        outbuf[f, y_rows(0), :] = start
        outbuf[f, y_rows(LY - 1), :] = end
        for k in range(1, LY - 1):
            outbuf[f, y_rows(k), :] = (
                inner[f, pl.ds(k * LX, LX), :] + first_ref[kind, k] * start + last_ref[kind, k] * end
            )
        copy = pltpu.make_async_copy(outbuf.at[f], out.at[f], out_sem.at[f])
        copy.start()
        outs.append(copy)

    pl.when(has_up)(x_up.wait_send)
    pl.when(has_down)(x_down.wait_send)
    pl.when(has_right)(y_up.wait_send)
    pl.when(has_left)(y_down.wait_send)
    departed(cxs, 0, PX, 8)
    departed(cys, 1, PY, 16)
    departed(xs, 2, PX, 8)
    departed(xb, 3, PX, 8)
    departed(ys, 4, PY, 16)
    departed(yb, 5, PY, 16)
    for copy in outs:
        copy.wait()


def per_device(flow_state, viscosity):
    f32 = jnp.float32
    vmem = lambda *shape: pltpu.VMEM(shape, f32)
    rows = LX * LY
    result = pl.pallas_call(
        kernel,
        out_shape=jax.ShapeDtypeStruct((NF, rows, NZ), f32),
        in_specs=[pl.BlockSpec(memory_space=pl.ANY)] * 2,
        out_specs=pl.BlockSpec(memory_space=pl.ANY),
        scratch_shapes=[
            vmem(NF, LX + 2, LY + 16, NZ),
            vmem(rows, NZ),
            vmem(NF, rows, NZ),
            vmem(NF, rows, NZ),
            vmem(NF, rows, NZ),
            *[vmem(2, LX, LY, NZ)] * 5,
            *[vmem(2, LY, LX, NZ)] * 5,
            *[vmem(PX + 1, 8, NZ)] * 3,
            *[vmem(PY + 1, 8, NZ)] * 6,
            *[vmem(8 * PX, NZ)] * 2,
            *[vmem(16 * PY, NZ)] * 2,
            *[vmem(8 * PX, NZ)] * 4,
            *[vmem(16 * PY, NZ)] * 4,
            pltpu.SemaphoreType.DMA((2,)),
            pltpu.SemaphoreType.DMA((NF,)),
            pltpu.SemaphoreType.DMA((6,)),
            pltpu.SemaphoreType.DMA((6,)),
            pltpu.SemaphoreType.DMA((4,)),
            pltpu.SemaphoreType.DMA((4,)),
        ],
        compiler_params=pltpu.CompilerParams(collective_id=0, has_side_effects=True),
    )(flow_state, viscosity.reshape(rows, NZ))
    return result.reshape(NF, LX, LY, NZ)


def solution(mesh):
    return jax.shard_map(
        per_device,
        mesh=mesh,
        in_specs=(P(None, "gx", "gy", None), P("gx", "gy", None)),
        out_specs=P(None, "gx", "gy", None),
        check_vma=False,
    )
```

```python
import jax
import jax.numpy as jnp
from jax import lax
from jax.experimental import pallas as pl
from jax.experimental.pallas import tpu as pltpu
from jax.sharding import PartitionSpec as P

MESH = pl.DeviceIdType.MESH

ADVECT = 0.2
BUOYANT = 0.5
CONDUCT = 0.6
KINDS = (1.0, CONDUCT)
KIND_OF = (0, 0, 0, 1)

NF = 4
LX, LY, NZ = 16, 32, 128
PX, PY = 32, 8
Y0 = 8


def factor(faces, along):
    inverse, lower, ratio = {}, {}, {}
    one = jnp.ones_like(faces[1])
    running = one
    forward = {}
    for k in range(1, along - 1):
        centre = 1.0 + faces[k] + faces[k + 1]
        if k > 1:
            centre = centre - faces[k] * ratio[k - 1]
        inverse[k] = 1.0 / centre
        lower[k] = faces[k] * inverse[k]
        ratio[k] = faces[k + 1] * inverse[k]
        running = lower[k] * running
        forward[k] = running
    first, last = {along - 1: jnp.zeros_like(one)}, {along - 1: one}
    for k in range(along - 2, 0, -1):
        first[k] = forward[k] + ratio[k] * first[k + 1]
        last[k] = ratio[k] * last[k + 1]
    first[0], last[0] = one, jnp.zeros_like(one)
    return inverse, lower, ratio, first, last


def keep_factor(load, along, keep, keep_ends, tiles):
    cells = [load(k) for k in range(along)]
    middles = [None] + [cells[k - 1] + cells[k] for k in range(1, along)]
    tiles[0] = cells[0]
    tiles[1] = cells[-1]
    for kind, scale in enumerate(KINDS):
        faces = [None] + [(0.5 * scale) * m for m in middles[1:]]
        inverse, lower, ratio, first, last = factor(faces, along)
        for k in range(1, along - 1):
            keep(kind, k, inverse[k], lower[k], ratio[k])
        for k in range(along):
            keep_ends(kind, k, first[k], last[k])
        tiles[2 + kind] = 1.0 + faces[1] * (1.0 - first[1])
        tiles[4 + kind] = faces[1] * last[1]
        tiles[6 + kind] = 1.0 + faces[along - 1] * (1.0 - last[along - 2])


def rolled(value):
    return pltpu.roll(value, 4, 0)


def interface_factor(coef, base, blocks, refs):
    inv_ref, low_ref, rat_ref = refs
    sub = lax.broadcasted_iota(jnp.int32, (8, NZ), 0)
    down = sub < 4
    thermal = (sub == 3) | (sub == 7)

    def row(block, r):
        return jnp.broadcast_to(coef[pl.ds(base(block) + r, 1), :], (8, NZ))

    def by_kind(block, r):
        return jnp.where(thermal, row(block, r + 1), row(block, r))

    scale = jnp.where(thermal, CONDUCT, 1.0).astype(jnp.float32)
    half = blocks // 2
    sides = []
    for i in range(half + 1):
        if i == 0:
            value = jnp.where(down, row(0, 0), row(blocks - 1, 1))
        elif i == half:
            value = 0.5 * (row(i - 1, 1) + row(i, 0))
        else:
            value = 0.5 * jnp.where(
                down,
                row(i - 1, 1) + row(i, 0),
                row(blocks - 1 - i, 1) + row(blocks - i, 0),
            )
        sides.append(scale * value)
    ratio = None
    for i in range(half):
        j = blocks - 1 - i
        couple = jnp.where(down, by_kind(i, 4), by_kind(j, 4))
        even = jnp.where(down, by_kind(i, 2), by_kind(j, 6)) + sides[i]
        odd = jnp.where(down, by_kind(i, 6), by_kind(j, 2)) + sides[i + 1]
        for m, centre, before, after in (
            (2 * i, even, sides[i], couple),
            (2 * i + 1, odd, couple, sides[i + 1]),
        ):
            if m > 0:
                centre = centre - before * ratio
            inverse = 1.0 / centre
            ratio = after * inverse
            inv_ref[m] = inverse
            low_ref[m] = before * inverse
            rat_ref[m] = ratio
    inv_ref[blocks] = 1.0 / (1.0 - ratio * rolled(ratio))


def interface_solve(right, solved, base, blocks, refs):
    inv_ref, low_ref, rat_ref = refs
    down = lax.broadcasted_iota(jnp.int32, (8, NZ), 0) < 4
    half = blocks // 2
    forward = []
    for i in range(half):
        j = blocks - 1 - i
        mine, other = right[pl.ds(base(i), 8), :], right[pl.ds(base(j), 8), :]
        even = jnp.where(down, mine, other)
        odd = rolled(jnp.where(down, other, mine))
        for m, value in ((2 * i, even), (2 * i + 1, odd)):
            value = inv_ref[m] * value
            if m > 0:
                value = value + low_ref[m] * forward[-1]
            forward.append(value)
    tail = forward[-1]
    values = [None] * blocks
    values[-1] = (tail + rat_ref[blocks - 1] * rolled(tail)) * inv_ref[blocks]
    for m in range(blocks - 2, -1, -1):
        values[m] = forward[m] + rat_ref[m] * values[m + 1]
    for i in range(half):
        j = blocks - 1 - i
        even, odd = values[2 * i], rolled(values[2 * i + 1])
        solved[pl.ds(base(i), 8), :] = jnp.where(down, even, odd)
        solved[pl.ds(base(j), 8), :] = jnp.where(down, odd, even)


def far_first(size_a, size_b):
    hops = lambda d, size: min(d, size - d)
    offsets = [(a, b) for a in range(size_a) for b in range(size_b) if (a, b) != (0, 0)]
    return sorted(offsets, key=lambda o: -hops(o[0], size_a) - hops(o[1], size_b))


def kernel(flow, visc, inner_y, first_y, last_y, yg, flat, vbuf, cur, inner, part, *rest):
    inv_x, low_x, rat_x, first_x, last_x = rest[0:5]
    inv_y, low_y, rat_y = rest[5:8]
    xi, yi = rest[8:11], (rest[11:14], rest[14:17])
    cxs, cxr, cys, cyr, xs, xr, xb, xg, ys, yr, yb = rest[17:28]
    xh_low, xh_high, yh_low, yh_high = rest[28:32]
    in_sem, send_sem, recv_sem, halo_send, halo_recv = rest[32:]
    gx, gy = lax.axis_index("gx"), lax.axis_index("gy")

    barrier = pltpu.get_barrier_semaphore()
    ring_z, cores = 8, 2
    ring_x, ring_y = PX // ring_z, PY // cores
    cx, cz = lax.div(gx, ring_z), lax.rem(gx, ring_z)
    cy, cc = lax.div(gy, cores), lax.rem(gy, cores)
    x_peers = [
        lax.rem(cx + dx, ring_x) * ring_z + lax.rem(cz + dz, ring_z)
        for dx, dz in far_first(ring_x, ring_z)
    ]
    y_peers = [
        lax.rem(cy + dy, ring_y) * cores + lax.rem(cc + dc, cores)
        for dy, dc in far_first(ring_y, cores)
    ]
    for peer in x_peers:
        pl.semaphore_signal(barrier, inc=1, device_id=(peer, gy), device_id_type=MESH)
    for peer in y_peers:
        pl.semaphore_signal(barrier, inc=1, device_id=(gx, peer), device_id_type=MESH)

    visc_in = pltpu.make_async_copy(visc, vbuf, in_sem.at[0])
    visc_in.start()
    wide = LY + 16

    def cells(k, shift=0):
        return pl.ds((k + 1) * wide + Y0 + shift, LY)

    flow_in = [
        pltpu.make_async_copy(flow.at[:, k], flat.at[:, cells(k), :], in_sem.at[1 + k])
        for k in range(LX)
    ]
    for copy in flow_in:
        copy.start()

    slab, edge = jnp.zeros((LY, NZ), jnp.float32), jnp.zeros((LX, NZ), jnp.float32)
    for f in range(NF):
        flat[f, cells(-1), :] = slab
        flat[f, cells(LX), :] = slab
        flat[f, pl.ds(wide + Y0 - 1, LX, stride=wide), :] = edge
        flat[f, pl.ds(wide + Y0 + LY, LX, stride=wide), :] = edge
        inner[f, pl.ds(0, LY), :] = slab
        inner[f, pl.ds((LX - 1) * LY, LY), :] = slab
        inner_y[f, pl.ds(0, LX, stride=LY), :] = edge
        inner_y[f, pl.ds(LY - 1, LX, stride=LY), :] = edge

    has_up, has_down = gx < PX - 1, gx > 0
    has_right, has_left = gy < PY - 1, gy > 0

    @pl.when(gx == 0)
    def _():
        xh_low[...] = jnp.zeros_like(xh_low)

    @pl.when(gx == PX - 1)
    def _():
        xh_high[...] = jnp.zeros_like(xh_high)

    @pl.when(gy == 0)
    def _():
        yh_low[...] = jnp.zeros_like(yh_low)

    @pl.when(gy == PY - 1)
    def _():
        yh_high[...] = jnp.zeros_like(yh_high)

    def x_rows(k):
        return pl.ds(pl.multiple_of(k * LY, 8), LY)

    def y_rows(k):
        return pl.ds(k, LX, stride=LY)

    def keep_x(kind, k, inverse, lower, ratio):
        inv_x[kind, x_rows(k), :] = inverse
        low_x[kind, x_rows(k), :] = lower
        rat_x[kind, x_rows(k), :] = ratio

    def keep_x_ends(kind, k, first, last):
        first_x[kind, x_rows(k), :] = first
        last_x[kind, x_rows(k), :] = last

    def keep_y(kind, k, inverse, lower, ratio):
        inv_y[kind, pl.ds(k * LX, LX), :] = inverse
        low_y[kind, pl.ds(k * LX, LX), :] = lower
        rat_y[kind, pl.ds(k * LX, LX), :] = ratio

    def keep_y_ends(kind, k, first, last):
        first_y[kind, y_rows(k), :] = first
        last_y[kind, y_rows(k), :] = last

    visc_in.wait()
    tiles = {}
    keep_factor(lambda k: vbuf[x_rows(k), :], LX, keep_x, keep_x_ends, tiles)
    for r in range(8):
        cxs[pl.ds(r, LY, stride=8), :] = tiles[r]

    for copy in flow_in:
        copy.wait()
    pl.semaphore_wait(barrier, PX - 1 + PY - 1)

    def halo(n, src, dst, device):
        return pltpu.make_async_remote_copy(
            src_ref=src,
            dst_ref=dst,
            send_sem=halo_send.at[n],
            recv_sem=halo_recv.at[n],
            device_id=device,
            device_id_type=MESH,
        )

    x_up = halo(0, flat.at[:, cells(LX - 1), :], xh_low, (lax.rem(gx + 1, PX), gy))
    x_down = halo(1, flat.at[:, cells(0), :], xh_high, (lax.rem(gx + PX - 1, PX), gy))
    y_up = halo(2, flow.at[:, :, LY - 1, :], yh_low, (gx, lax.rem(gy + 1, PY)))
    y_down = halo(3, flow.at[:, :, 0, :], yh_high, (gx, lax.rem(gy + PY - 1, PY)))
    pl.when(has_up)(x_up.start)
    pl.when(has_down)(x_down.start)
    pl.when(has_right)(y_up.start)
    pl.when(has_left)(y_down.start)

    def spread(src, dst, n, along_x, size):
        peers, me = (x_peers, gx) if along_x else (y_peers, gy)
        mine = pl.ds(pl.multiple_of(me * size, 8), size)
        for peer in peers:
            pltpu.make_async_remote_copy(
                src_ref=src.at[pl.ds(pl.multiple_of(peer * size, 8), size), :],
                dst_ref=dst.at[mine, :],
                send_sem=send_sem.at[n],
                recv_sem=recv_sem.at[n],
                device_id=(peer, gy) if along_x else (gx, peer),
                device_id_type=MESH,
            ).start()
        dst[mine, :] = src[mine, :]

    def arrived(dst, n, peers, size):
        piece = dst.at[pl.ds(0, (peers - 1) * size), :]
        pltpu.make_async_copy(piece, piece, recv_sem.at[n]).wait()

    def departed(src, n, peers, size):
        piece = src.at[pl.ds(0, (peers - 1) * size), :]
        pltpu.make_async_copy(piece, piece, send_sem.at[n]).wait()

    spread(cxs, cxr, 0, True, 8)

    def source_row(k, sums):
        here = [flat[f, cells(k), :] for f in range(NF)]
        firsts, lasts = [], []
        for f in range(NF):
            across_x = flat[f, cells(k + 1), :] - flat[f, cells(k - 1), :]
            across_y = flat[f, cells(k, 1), :] - flat[f, cells(k, -1), :]
            across_z = pltpu.roll(here[f], NZ - 1, 1) - pltpu.roll(here[f], 1, 1)
            carried = here[0] * across_x + here[1] * across_y + here[2] * across_z
            source = here[f] - (0.5 * ADVECT) * carried
            if f == 2:
                source = source + BUOYANT * here[3]
            cur[f, x_rows(k), :] = source
            kind = KIND_OF[f]
            firsts.append(sums[f] + first_x[kind, x_rows(k), :] * source)
            lasts.append(sums[NF + f] + last_x[kind, x_rows(k), :] * source)
        return tuple(firsts + lasts)

    sums = (slab,) * (2 * NF)
    for k in range(LX):
        sums = source_row(k, sums)
    for r in range(8):
        xs[pl.ds(r, LY, stride=8), :] = sums[r]

    tiles = {}
    keep_factor(lambda k: vbuf[y_rows(k), :], LY, keep_y, keep_y_ends, tiles)
    for r in range(8):
        cys[pl.ds(r, LX, stride=8), :] = tiles[r]
    spread(cys, cyr, 1, False, 16)

    half = 0.5 * ADVECT
    pl.when(has_left)(y_up.wait_recv)
    pl.when(has_right)(y_down.wait_recv)
    for at, around, sign in ((0, yh_low, half), (LY - 1, yh_high, -half)):
        speed = sign * flat[1, pl.ds(wide + Y0 + at, LX, stride=wide), :]
        for f in range(NF):
            kind = KIND_OF[f]
            change = speed * around[f]
            cur[f, y_rows(at), :] = cur[f, y_rows(at), :] + change
            for r, weight in ((f, first_x), (NF + f, last_x)):
                row = pl.ds(at * 8 + r, 1)
                total = jnp.sum(weight[kind, y_rows(at), :] * change, axis=0, keepdims=True)
                xs[row, :] = xs[row, :] + total
    pl.when(has_down)(x_up.wait_recv)
    pl.when(has_up)(x_down.wait_recv)
    for r, at, around, sign in ((0, 0, xh_low, half), (NF, LX - 1, xh_high, -half)):
        speed = sign * flat[0, cells(at), :]
        for f in range(NF):
            row = pl.ds(r + f, LY, stride=8)
            xs[row, :] = xs[row, :] + speed * around[f]
    spread(xs, xr, 2, True, 8)

    def x_down_row(k, before):
        result = []
        for f in range(NF):
            kind = KIND_OF[f]
            value = inv_x[kind, x_rows(k), :] * cur[f, x_rows(k), :] + low_x[kind, x_rows(k), :] * before[f]
            inner[f, x_rows(k), :] = value
            result.append(value)
        return tuple(result)

    def x_up_row(step, after):
        k = LX - 3 - step
        result = []
        for f in range(NF):
            value = inner[f, x_rows(k), :] + rat_x[KIND_OF[f], x_rows(k), :] * after[f]
            inner[f, x_rows(k), :] = value
            result.append(value)
        return tuple(result)

    tail = lax.fori_loop(1, LX - 1, x_down_row, (slab,) * NF)
    lax.fori_loop(0, LX - 3, x_up_row, tail)

    arrived(cxr, 0, PX, 8)
    interface_factor(cxr, lambda b: 8 * b, PX, xi)
    arrived(cyr, 1, PY, 16)
    for t in range(2):
        interface_factor(cyr, lambda b, t=t: 16 * b + 8 * t, PY, yi[t])

    arrived(xr, 2, PX, 8)
    interface_solve(xr, xb, lambda b: 8 * b, PX, xi)
    spread(xb, xg, 3, True, 8)
    arrived(xg, 3, PX, 8)

    for f in range(NF):
        kind = KIND_OF[f]
        start, end = xg[pl.ds(f, LY, stride=8), :], xg[pl.ds(NF + f, LY, stride=8), :]

        def x_row(k, carry, f=f, kind=kind, start=start, end=end):
            rows = x_rows(k)
            value = inner[f, rows, :] + first_x[kind, rows, :] * start + last_x[kind, rows, :] * end
            cur[f, rows, :] = value
            for r, weight in ((f, first_y), (NF + f, last_y)):
                share = weight[kind, rows, :] * value
                total = share[0:8]
                for q in range(8, LY, 8):
                    total = total + share[q : q + 8]
                part[pl.ds(pl.multiple_of(k * 64, 8) + 8 * r, 8), :] = total
            return carry

        lax.fori_loop(0, LX, x_row, 0, unroll=4)
    for k in range(LX):
        total = part[pl.ds(64 * k, 8, stride=8), :]
        for q in range(1, 8):
            total = total + part[pl.ds(64 * k + q, 8, stride=8), :]
        ys[pl.ds(8 * k, 8), :] = total
    spread(ys, yr, 4, False, 16)

    before = [edge] * NF
    for k in range(1, LY - 1):
        rows = pl.ds(k * LX, LX)
        for f in range(NF):
            kind = KIND_OF[f]
            before[f] = inv_y[kind, rows, :] * cur[f, y_rows(k), :] + low_y[kind, rows, :] * before[f]
            inner[f, rows, :] = before[f]
    after = before
    for f in range(NF):
        inner_y[f, y_rows(LY - 2), :] = after[f]
    for k in range(LY - 3, 0, -1):
        rows = pl.ds(k * LX, LX)
        for f in range(NF):
            after[f] = inner[f, rows, :] + rat_y[KIND_OF[f], rows, :] * after[f]
            inner_y[f, y_rows(k), :] = after[f]

    arrived(yr, 4, PY, 16)
    for t in range(2):
        interface_solve(yr, yb, lambda b, t=t: 16 * b + 8 * t, PY, yi[t])
    spread(yb, yg, 5, False, 16)

    pl.when(has_up)(x_up.wait_send)
    pl.when(has_down)(x_down.wait_send)
    pl.when(has_right)(y_up.wait_send)
    pl.when(has_left)(y_down.wait_send)
    departed(cxs, 0, PX, 8)
    departed(cys, 1, PY, 16)
    departed(xs, 2, PX, 8)
    departed(xb, 3, PX, 8)
    departed(ys, 4, PY, 16)
    departed(yb, 5, PY, 16)
    arrived(yg, 5, PY, 16)


CHUNK = 4


def assemble(inner, first, last, ends, out, done, sem):
    copies = []
    for k in range(LX):
        rows = pl.ds(k * LY, LY)
        for f in range(NF):
            kind = KIND_OF[f]
            done[f, rows, :] = (
                inner[f, rows, :]
                + first[kind, rows, :] * ends[pl.ds(8 * k + f, 1), :]
                + last[kind, rows, :] * ends[pl.ds(8 * k + NF + f, 1), :]
            )
        if k % CHUNK == CHUNK - 1:
            rows = pl.ds((k + 1 - CHUNK) * LY, CHUNK * LY)
            copies.append(
                pltpu.make_async_copy(done.at[:, rows, :], out.at[:, rows, :], sem.at[k // CHUNK])
            )
            copies[-1].start()
    for copy in copies:
        copy.wait()


def per_device(flow_state, viscosity):
    f32 = jnp.float32
    vmem = lambda *shape: pltpu.VMEM(shape, f32)
    rows = LX * LY
    in_vmem = pl.BlockSpec(memory_space=pltpu.VMEM)
    kept = pl.pallas_call(
        kernel,
        out_shape=[
            vmem(NF, rows, NZ),
            vmem(2, rows, NZ),
            vmem(2, rows, NZ),
            vmem(16 * PY, NZ),
        ],
        in_specs=[pl.BlockSpec(memory_space=pl.ANY)] * 2,
        out_specs=[in_vmem] * 4,
        scratch_shapes=[
            vmem(NF, (LX + 2) * (LY + 16), NZ),
            vmem(rows, NZ),
            vmem(NF, rows, NZ),
            vmem(NF, rows, NZ),
            vmem(LX * 64, NZ),
            *[vmem(2, rows, NZ)] * 8,
            *[vmem(PX + 1, 8, NZ)] * 3,
            *[vmem(PY + 1, 8, NZ)] * 6,
            *[vmem(8 * PX, NZ)] * 2,
            *[vmem(16 * PY, NZ)] * 2,
            *[vmem(8 * PX, NZ)] * 4,
            *[vmem(16 * PY, NZ)] * 3,
            *[vmem(NF, LY, NZ)] * 2,
            *[vmem(NF, LX, NZ)] * 2,
            pltpu.SemaphoreType.DMA((1 + LX,)),
            pltpu.SemaphoreType.DMA((6,)),
            pltpu.SemaphoreType.DMA((6,)),
            pltpu.SemaphoreType.DMA((4,)),
            pltpu.SemaphoreType.DMA((4,)),
        ],
        compiler_params=pltpu.CompilerParams(collective_id=0, has_side_effects=True),
    )(flow_state, viscosity.reshape(rows, NZ))
    result = pl.pallas_call(
        assemble,
        out_shape=jax.ShapeDtypeStruct((NF, rows, NZ), f32),
        in_specs=[in_vmem] * 4,
        out_specs=pl.BlockSpec(memory_space=pl.ANY),
        scratch_shapes=[vmem(NF, rows, NZ), pltpu.SemaphoreType.DMA((LX // CHUNK,))],
        compiler_params=pltpu.CompilerParams(vmem_limit_bytes=8 << 20),
    )(*kept)
    return result.reshape(NF, LX, LY, NZ)


def solution(mesh):
    return jax.shard_map(
        per_device,
        mesh=mesh,
        in_specs=(P(None, "gx", "gy", None), P("gx", "gy", None)),
        out_specs=P(None, "gx", "gy", None),
        check_vma=False,
    )
```

```python
import jax
import jax.numpy as jnp
from jax import lax
from jax.experimental import pallas as pl
from jax.experimental.pallas import tpu as pltpu
from jax.sharding import PartitionSpec as P

MESH = pl.DeviceIdType.MESH

ADVECT = 0.2
BUOYANT = 0.5
CONDUCT = 0.6
KINDS = (1.0, CONDUCT)
KIND_OF = (0, 0, 0, 1)

NF = 4
LX, LY, NZ = 16, 32, 128
PX, PY = 32, 8
Y0 = 8
STAGES = 6


def factor(faces, along):
    inverse, lower, ratio = {}, {}, {}
    one = jnp.ones_like(faces[1])
    running = one
    forward = {}
    for k in range(1, along - 1):
        centre = 1.0 + faces[k] + faces[k + 1]
        if k > 1:
            centre = centre - faces[k] * ratio[k - 1]
        inverse[k] = 1.0 / centre
        lower[k] = faces[k] * inverse[k]
        ratio[k] = faces[k + 1] * inverse[k]
        running = lower[k] * running
        forward[k] = running
    first, last = {along - 1: jnp.zeros_like(one)}, {along - 1: one}
    for k in range(along - 2, 0, -1):
        first[k] = forward[k] + ratio[k] * first[k + 1]
        last[k] = ratio[k] * last[k + 1]
    first[0], last[0] = one, jnp.zeros_like(one)
    return inverse, lower, ratio, first, last


def keep_factor(load, along, keep, keep_ends, tiles):
    cells = [load(k) for k in range(along)]
    middles = [None] + [cells[k - 1] + cells[k] for k in range(1, along)]
    tiles[0] = cells[0]
    tiles[1] = cells[-1]
    for kind, scale in enumerate(KINDS):
        faces = [None] + [(0.5 * scale) * m for m in middles[1:]]
        inverse, lower, ratio, first, last = factor(faces, along)
        for k in range(1, along - 1):
            keep(kind, k, inverse[k], lower[k], ratio[k])
        for k in range(along):
            keep_ends(kind, k, first[k], last[k])
        tiles[2 + kind] = 1.0 + faces[1] * (1.0 - first[1])
        tiles[4 + kind] = faces[1] * last[1]
        tiles[6 + kind] = 1.0 + faces[along - 1] * (1.0 - last[along - 2])


def rolled(value):
    return pltpu.roll(value, 4, 0)


def interface_factor(coef, base, blocks, refs):
    inv_ref, low_ref, rat_ref = refs
    sub = lax.broadcasted_iota(jnp.int32, (8, NZ), 0)
    down = sub < 4
    thermal = (sub == 3) | (sub == 7)

    def row(block, r):
        return jnp.broadcast_to(coef[pl.ds(base(block) + r, 1), :], (8, NZ))

    def by_kind(block, r):
        return jnp.where(thermal, row(block, r + 1), row(block, r))

    scale = jnp.where(thermal, CONDUCT, 1.0).astype(jnp.float32)
    half = blocks // 2
    sides = []
    for i in range(half + 1):
        if i == 0:
            value = jnp.where(down, row(0, 0), row(blocks - 1, 1))
        elif i == half:
            value = 0.5 * (row(i - 1, 1) + row(i, 0))
        else:
            value = 0.5 * jnp.where(
                down,
                row(i - 1, 1) + row(i, 0),
                row(blocks - 1 - i, 1) + row(blocks - i, 0),
            )
        sides.append(scale * value)
    ratio = None
    for i in range(half):
        j = blocks - 1 - i
        couple = jnp.where(down, by_kind(i, 4), by_kind(j, 4))
        even = jnp.where(down, by_kind(i, 2), by_kind(j, 6)) + sides[i]
        odd = jnp.where(down, by_kind(i, 6), by_kind(j, 2)) + sides[i + 1]
        for m, centre, before, after in (
            (2 * i, even, sides[i], couple),
            (2 * i + 1, odd, couple, sides[i + 1]),
        ):
            if m > 0:
                centre = centre - before * ratio
            inverse = 1.0 / centre
            ratio = after * inverse
            inv_ref[m] = inverse
            low_ref[m] = before * inverse
            rat_ref[m] = ratio
    inv_ref[blocks] = 1.0 / (1.0 - ratio * rolled(ratio))


def interface_solve(right, solved, base, blocks, refs):
    inv_ref, low_ref, rat_ref = refs
    down = lax.broadcasted_iota(jnp.int32, (8, NZ), 0) < 4
    half = blocks // 2
    forward = []
    for i in range(half):
        j = blocks - 1 - i
        mine, other = right[pl.ds(base(i), 8), :], right[pl.ds(base(j), 8), :]
        even = jnp.where(down, mine, other)
        odd = rolled(jnp.where(down, other, mine))
        for m, value in ((2 * i, even), (2 * i + 1, odd)):
            value = inv_ref[m] * value
            if m > 0:
                value = value + low_ref[m] * forward[-1]
            forward.append(value)
    tail = forward[-1]
    values = [None] * blocks
    values[-1] = (tail + rat_ref[blocks - 1] * rolled(tail)) * inv_ref[blocks]
    for m in range(blocks - 2, -1, -1):
        values[m] = forward[m] + rat_ref[m] * values[m + 1]
    for i in range(half):
        j = blocks - 1 - i
        even, odd = values[2 * i], rolled(values[2 * i + 1])
        solved[pl.ds(base(i), 8), :] = jnp.where(down, even, odd)
        solved[pl.ds(base(j), 8), :] = jnp.where(down, odd, even)


def far_first(size_a, size_b):
    hops = lambda a, b: min(a, size_a - a) + min(b, size_b - b)
    offsets = [(a, b, hops(a, b)) for a in range(size_a) for b in range(size_b) if (a, b) != (0, 0)]
    return sorted(offsets, key=lambda o: -o[2])


def beside(size):
    return sorted({1 % size, size - 1} - {0})


def kernel(flow, visc, inner_y, first_y, last_y, yg, flat, vbuf, cur, inner, part, *rest):
    inv_x, low_x, rat_x, first_x, last_x = rest[0:5]
    inv_y, low_y, rat_y = rest[5:8]
    xi, yi = rest[8:11], (rest[11:14], rest[14:17])
    cxs, cxr, cys, cyr, xs, xr, xb, xg, ys, yr, yb = rest[17:28]
    xh_low, xh_high, yh_low, yh_high = rest[28:32]
    in_sem, send_sem, recv_sem, halo_send, halo_recv, meet = rest[32:]
    gx, gy = lax.axis_index("gx"), lax.axis_index("gy")

    barrier = pltpu.get_barrier_semaphore()
    ring_z, cores = 8, 2
    ring_x, ring_y = PX // ring_z, PY // cores
    cx, cz = lax.div(gx, ring_z), lax.rem(gx, ring_z)
    cy, cc = lax.div(gy, cores), lax.rem(gy, cores)
    x_peers = [
        (lax.rem(cx + dx, ring_x) * ring_z + lax.rem(cz + dz, ring_z), hops)
        for dx, dz, hops in far_first(ring_x, ring_z)
    ]
    y_peers = [
        (lax.rem(cy + dy, ring_y) * cores + lax.rem(cc + dc, cores), hops)
        for dy, dc, hops in far_first(ring_y, cores)
    ]
    up, down = (lax.rem(gx + 1, PX), gy), (lax.rem(gx + PX - 1, PX), gy)
    right, left = (gx, lax.rem(gy + 1, PY)), (gx, lax.rem(gy + PY - 1, PY))
    has_up, has_down = gx < PX - 1, gx > 0
    has_right, has_left = gy < PY - 1, gy > 0

    neighbours = (
        [(cx * ring_z + lax.rem(cz + d, ring_z), gy) for d in beside(ring_z)]
        + [(lax.rem(cx + d, ring_x) * ring_z + cz, gy) for d in beside(ring_x)]
        + [(gx, lax.rem(gy + d, PY)) for d in beside(PY)]
    )
    crosses_up = has_up & (cz == ring_z - 1)
    crosses_down = has_down & (cz == 0)

    def greet(sem):
        for device in neighbours:
            pl.semaphore_signal(sem, inc=1, device_id=device, device_id_type=MESH)

    def met(stage):
        pl.semaphore_wait(meet.at[stage - 2], len(neighbours))
        if stage < STAGES:
            greet(meet.at[stage - 1])

    greet(barrier)

    @pl.when(crosses_up)
    def _():
        pl.semaphore_signal(barrier, inc=1, device_id=up, device_id_type=MESH)

    @pl.when(crosses_down)
    def _():
        pl.semaphore_signal(barrier, inc=1, device_id=down, device_id_type=MESH)

    visc_in = pltpu.make_async_copy(visc, vbuf, in_sem.at[0])
    visc_in.start()
    wide = LY + 16

    def cells(k, shift=0):
        return pl.ds((k + 1) * wide + Y0 + shift, LY)

    flow_in = [
        pltpu.make_async_copy(flow.at[:, k], flat.at[:, cells(k), :], in_sem.at[1 + k])
        for k in range(LX)
    ]
    for copy in flow_in:
        copy.start()

    slab, edge = jnp.zeros((LY, NZ), jnp.float32), jnp.zeros((LX, NZ), jnp.float32)
    for f in range(NF):
        flat[f, cells(-1), :] = slab
        flat[f, cells(LX), :] = slab
        flat[f, pl.ds(wide + Y0 - 1, LX, stride=wide), :] = edge
        flat[f, pl.ds(wide + Y0 + LY, LX, stride=wide), :] = edge
        inner[f, pl.ds(0, LY), :] = slab
        inner[f, pl.ds((LX - 1) * LY, LY), :] = slab
        inner_y[f, pl.ds(0, LX, stride=LY), :] = edge
        inner_y[f, pl.ds(LY - 1, LX, stride=LY), :] = edge

    @pl.when(gx == 0)
    def _():
        xh_low[...] = jnp.zeros_like(xh_low)

    @pl.when(gx == PX - 1)
    def _():
        xh_high[...] = jnp.zeros_like(xh_high)

    @pl.when(gy == 0)
    def _():
        yh_low[...] = jnp.zeros_like(yh_low)

    @pl.when(gy == PY - 1)
    def _():
        yh_high[...] = jnp.zeros_like(yh_high)

    crossings = crosses_up.astype(jnp.int32) + crosses_down.astype(jnp.int32)
    pl.semaphore_wait(barrier, len(neighbours) + crossings)

    def halo(n, src, dst, device):
        return pltpu.make_async_remote_copy(
            src_ref=src,
            dst_ref=dst,
            send_sem=halo_send.at[n],
            recv_sem=halo_recv.at[n],
            device_id=device,
            device_id_type=MESH,
        )

    x_up = halo(0, flow.at[:, LX - 1], xh_low, up)
    x_down = halo(1, flow.at[:, 0], xh_high, down)
    y_up = halo(2, flow.at[:, :, LY - 1, :], yh_low, right)
    y_down = halo(3, flow.at[:, :, 0, :], yh_high, left)
    pl.when(has_up)(x_up.start)
    pl.when(has_down)(x_down.start)
    pl.when(has_right)(y_up.start)
    pl.when(has_left)(y_down.start)
    greet(meet.at[0])

    def x_rows(k):
        return pl.ds(pl.multiple_of(k * LY, 8), LY)

    def y_rows(k):
        return pl.ds(k, LX, stride=LY)

    def keep_x(kind, k, inverse, lower, ratio):
        inv_x[kind, x_rows(k), :] = inverse
        low_x[kind, x_rows(k), :] = lower
        rat_x[kind, x_rows(k), :] = ratio

    def keep_x_ends(kind, k, first, last):
        first_x[kind, x_rows(k), :] = first
        last_x[kind, x_rows(k), :] = last

    def keep_y(kind, k, inverse, lower, ratio):
        inv_y[kind, pl.ds(k * LX, LX), :] = inverse
        low_y[kind, pl.ds(k * LX, LX), :] = lower
        rat_y[kind, pl.ds(k * LX, LX), :] = ratio

    def keep_y_ends(kind, k, first, last):
        first_y[kind, y_rows(k), :] = first
        last_y[kind, y_rows(k), :] = last

    visc_in.wait()
    tiles = {}
    keep_factor(lambda k: vbuf[x_rows(k), :], LX, keep_x, keep_x_ends, tiles)
    for r in range(8):
        cxs[pl.ds(r, LY, stride=8), :] = tiles[r]

    def spread(src, dst, n, along_x, size, least=1, most=99):
        peers, me = (x_peers, gx) if along_x else (y_peers, gy)
        mine = pl.ds(pl.multiple_of(me * size, 8), size)
        for peer, hops in peers:
            if least <= hops <= most:
                pltpu.make_async_remote_copy(
                    src_ref=src.at[pl.ds(pl.multiple_of(peer * size, 8), size), :],
                    dst_ref=dst.at[mine, :],
                    send_sem=send_sem.at[n],
                    recv_sem=recv_sem.at[n],
                    device_id=(peer, gy) if along_x else (gx, peer),
                    device_id_type=MESH,
                ).start()
        if least <= 1:
            dst[mine, :] = src[mine, :]

    def arrived(dst, n, peers, size):
        piece = dst.at[pl.ds(0, (peers - 1) * size), :]
        pltpu.make_async_copy(piece, piece, recv_sem.at[n]).wait()

    def departed(src, n, peers, size):
        piece = src.at[pl.ds(0, (peers - 1) * size), :]
        pltpu.make_async_copy(piece, piece, send_sem.at[n]).wait()

    met(2)
    spread(cxs, cxr, 0, True, 8, 1, 2)
    for copy in flow_in:
        copy.wait()

    def source_row(k, sums):
        here = [flat[f, cells(k), :] for f in range(NF)]
        firsts, lasts = [], []
        for f in range(NF):
            across_x = flat[f, cells(k + 1), :] - flat[f, cells(k - 1), :]
            across_y = flat[f, cells(k, 1), :] - flat[f, cells(k, -1), :]
            across_z = pltpu.roll(here[f], NZ - 1, 1) - pltpu.roll(here[f], 1, 1)
            carried = here[0] * across_x + here[1] * across_y + here[2] * across_z
            source = here[f] - (0.5 * ADVECT) * carried
            if f == 2:
                source = source + BUOYANT * here[3]
            cur[f, x_rows(k), :] = source
            kind = KIND_OF[f]
            firsts.append(sums[f] + first_x[kind, x_rows(k), :] * source)
            lasts.append(sums[NF + f] + last_x[kind, x_rows(k), :] * source)
        return tuple(firsts + lasts)

    sums = (slab,) * (2 * NF)
    for k in range(LX):
        sums = source_row(k, sums)
    for r in range(8):
        xs[pl.ds(r, LY, stride=8), :] = sums[r]

    for stage in range(3, STAGES):
        met(stage)
        spread(cxs, cxr, 0, True, 8, stage, stage)

    half = 0.5 * ADVECT
    pl.when(has_left)(y_up.wait_recv)
    pl.when(has_right)(y_down.wait_recv)
    for at, around, sign in ((0, yh_low, half), (LY - 1, yh_high, -half)):
        speed = sign * flat[1, pl.ds(wide + Y0 + at, LX, stride=wide), :]
        for f in range(NF):
            kind = KIND_OF[f]
            change = speed * around[f]
            cur[f, y_rows(at), :] = cur[f, y_rows(at), :] + change
            for r, weight in ((f, first_x), (NF + f, last_x)):
                row = pl.ds(at * 8 + r, 1)
                total = jnp.sum(weight[kind, y_rows(at), :] * change, axis=0, keepdims=True)
                xs[row, :] = xs[row, :] + total
    pl.when(has_down)(x_up.wait_recv)
    pl.when(has_up)(x_down.wait_recv)
    for r, at, around, sign in ((0, 0, xh_low, half), (NF, LX - 1, xh_high, -half)):
        speed = sign * flat[0, cells(at), :]
        for f in range(NF):
            row = pl.ds(r + f, LY, stride=8)
            xs[row, :] = xs[row, :] + speed * around[f]
    met(STAGES)
    spread(xs, xr, 2, True, 8)
    spread(cxs, cxr, 0, True, 8, STAGES)

    def x_down_row(k, before):
        result = []
        for f in range(NF):
            kind = KIND_OF[f]
            value = inv_x[kind, x_rows(k), :] * cur[f, x_rows(k), :] + low_x[kind, x_rows(k), :] * before[f]
            inner[f, x_rows(k), :] = value
            result.append(value)
        return tuple(result)

    def x_up_row(step, after):
        k = LX - 3 - step
        result = []
        for f in range(NF):
            value = inner[f, x_rows(k), :] + rat_x[KIND_OF[f], x_rows(k), :] * after[f]
            inner[f, x_rows(k), :] = value
            result.append(value)
        return tuple(result)

    tail = lax.fori_loop(1, LX - 1, x_down_row, (slab,) * NF)
    lax.fori_loop(0, LX - 3, x_up_row, tail)

    tiles = {}
    keep_factor(lambda k: vbuf[y_rows(k), :], LY, keep_y, keep_y_ends, tiles)
    for r in range(8):
        cys[pl.ds(r, LX, stride=8), :] = tiles[r]
    spread(cys, cyr, 1, False, 16)

    arrived(cxr, 0, PX, 8)
    interface_factor(cxr, lambda b: 8 * b, PX, xi)
    arrived(xr, 2, PX, 8)
    interface_solve(xr, xb, lambda b: 8 * b, PX, xi)
    spread(xb, xg, 3, True, 8)
    arrived(cyr, 1, PY, 16)
    for t in range(2):
        interface_factor(cyr, lambda b, t=t: 16 * b + 8 * t, PY, yi[t])
    arrived(xg, 3, PX, 8)

    for f in range(NF):
        kind = KIND_OF[f]
        start, end = xg[pl.ds(f, LY, stride=8), :], xg[pl.ds(NF + f, LY, stride=8), :]

        def x_row(k, carry, f=f, kind=kind, start=start, end=end):
            rows = x_rows(k)
            value = inner[f, rows, :] + first_x[kind, rows, :] * start + last_x[kind, rows, :] * end
            cur[f, rows, :] = value
            for r, weight in ((f, first_y), (NF + f, last_y)):
                share = weight[kind, rows, :] * value
                total = share[0:8]
                for q in range(8, LY, 8):
                    total = total + share[q : q + 8]
                part[pl.ds(pl.multiple_of(k * 64, 8) + 8 * r, 8), :] = total
            return carry

        lax.fori_loop(0, LX, x_row, 0, unroll=4)
    for k in range(LX):
        total = part[pl.ds(64 * k, 8, stride=8), :]
        for q in range(1, 8):
            total = total + part[pl.ds(64 * k + q, 8, stride=8), :]
        ys[pl.ds(8 * k, 8), :] = total
    spread(ys, yr, 4, False, 16)

    before = [edge] * NF
    for k in range(1, LY - 1):
        rows = pl.ds(k * LX, LX)
        for f in range(NF):
            kind = KIND_OF[f]
            before[f] = inv_y[kind, rows, :] * cur[f, y_rows(k), :] + low_y[kind, rows, :] * before[f]
            inner[f, rows, :] = before[f]
    after = before
    for f in range(NF):
        inner_y[f, y_rows(LY - 2), :] = after[f]
    for k in range(LY - 3, 0, -1):
        rows = pl.ds(k * LX, LX)
        for f in range(NF):
            after[f] = inner[f, rows, :] + rat_y[KIND_OF[f], rows, :] * after[f]
            inner_y[f, y_rows(k), :] = after[f]

    arrived(yr, 4, PY, 16)
    for t in range(2):
        interface_solve(yr, yb, lambda b, t=t: 16 * b + 8 * t, PY, yi[t])
    spread(yb, yg, 5, False, 16)

    pl.when(has_up)(x_up.wait_send)
    pl.when(has_down)(x_down.wait_send)
    pl.when(has_right)(y_up.wait_send)
    pl.when(has_left)(y_down.wait_send)
    departed(cxs, 0, PX, 8)
    departed(cys, 1, PY, 16)
    departed(xs, 2, PX, 8)
    departed(xb, 3, PX, 8)
    departed(ys, 4, PY, 16)
    departed(yb, 5, PY, 16)
    arrived(yg, 5, PY, 16)


CHUNK = 4


def assemble(inner, first, last, ends, out, done, sem):
    copies = []
    for k in range(LX):
        rows = pl.ds(k * LY, LY)
        for f in range(NF):
            kind = KIND_OF[f]
            done[f, rows, :] = (
                inner[f, rows, :]
                + first[kind, rows, :] * ends[pl.ds(8 * k + f, 1), :]
                + last[kind, rows, :] * ends[pl.ds(8 * k + NF + f, 1), :]
            )
        if k % CHUNK == CHUNK - 1:
            rows = pl.ds((k + 1 - CHUNK) * LY, CHUNK * LY)
            copies.append(
                pltpu.make_async_copy(done.at[:, rows, :], out.at[:, rows, :], sem.at[k // CHUNK])
            )
            copies[-1].start()
    for copy in copies:
        copy.wait()


def per_device(flow_state, viscosity):
    f32 = jnp.float32
    vmem = lambda *shape: pltpu.VMEM(shape, f32)
    rows = LX * LY
    in_vmem = pl.BlockSpec(memory_space=pltpu.VMEM)
    kept = pl.pallas_call(
        kernel,
        out_shape=[
            vmem(NF, rows, NZ),
            vmem(2, rows, NZ),
            vmem(2, rows, NZ),
            vmem(16 * PY, NZ),
        ],
        in_specs=[pl.BlockSpec(memory_space=pl.ANY)] * 2,
        out_specs=[in_vmem] * 4,
        scratch_shapes=[
            vmem(NF, (LX + 2) * (LY + 16), NZ),
            vmem(rows, NZ),
            vmem(NF, rows, NZ),
            vmem(NF, rows, NZ),
            vmem(LX * 64, NZ),
            *[vmem(2, rows, NZ)] * 8,
            *[vmem(PX + 1, 8, NZ)] * 3,
            *[vmem(PY + 1, 8, NZ)] * 6,
            *[vmem(8 * PX, NZ)] * 2,
            *[vmem(16 * PY, NZ)] * 2,
            *[vmem(8 * PX, NZ)] * 4,
            *[vmem(16 * PY, NZ)] * 3,
            *[vmem(NF, LY, NZ)] * 2,
            *[vmem(NF, LX, NZ)] * 2,
            pltpu.SemaphoreType.DMA((1 + LX,)),
            pltpu.SemaphoreType.DMA((6,)),
            pltpu.SemaphoreType.DMA((6,)),
            pltpu.SemaphoreType.DMA((4,)),
            pltpu.SemaphoreType.DMA((4,)),
            pltpu.SemaphoreType.REGULAR((STAGES - 1,)),
        ],
        compiler_params=pltpu.CompilerParams(collective_id=0, has_side_effects=True),
    )(flow_state, viscosity.reshape(rows, NZ))
    result = pl.pallas_call(
        assemble,
        out_shape=jax.ShapeDtypeStruct((NF, rows, NZ), f32),
        in_specs=[in_vmem] * 4,
        out_specs=pl.BlockSpec(memory_space=pl.ANY),
        scratch_shapes=[vmem(NF, rows, NZ), pltpu.SemaphoreType.DMA((LX // CHUNK,))],
        compiler_params=pltpu.CompilerParams(vmem_limit_bytes=8 << 20),
    )(*kept)
    return result.reshape(NF, LX, LY, NZ)


def solution(mesh):
    return jax.shard_map(
        per_device,
        mesh=mesh,
        in_specs=(P(None, "gx", "gy", None), P("gx", "gy", None)),
        out_specs=P(None, "gx", "gy", None),
        check_vma=False,
    )
```

```python
import jax
import jax.numpy as jnp
from jax import lax
from jax.experimental import pallas as pl
from jax.experimental.pallas import tpu as pltpu
from jax.sharding import PartitionSpec as P

MESH = pl.DeviceIdType.MESH

ADVECT = 0.2
BUOYANT = 0.5
CONDUCT = 0.6
KINDS = (1.0, CONDUCT)
KIND_OF = (0, 0, 0, 1)

NF = 4
LX, LY, NZ = 16, 32, 128
PX, PY = 32, 8
Y0 = 8


def factor(faces, along):
    inverse, lower, ratio = {}, {}, {}
    one = jnp.ones_like(faces[1])
    running = one
    forward = {}
    for k in range(1, along - 1):
        centre = 1.0 + faces[k] + faces[k + 1]
        if k > 1:
            centre = centre - faces[k] * ratio[k - 1]
        inverse[k] = 1.0 / centre
        lower[k] = faces[k] * inverse[k]
        ratio[k] = faces[k + 1] * inverse[k]
        running = lower[k] * running
        forward[k] = running
    first, last = {along - 1: jnp.zeros_like(one)}, {along - 1: one}
    for k in range(along - 2, 0, -1):
        first[k] = forward[k] + ratio[k] * first[k + 1]
        last[k] = ratio[k] * last[k + 1]
    first[0], last[0] = one, jnp.zeros_like(one)
    return inverse, lower, ratio, first, last


def keep_factor(load, along, keep, keep_ends, tiles):
    cells = [load(k) for k in range(along)]
    middles = [None] + [cells[k - 1] + cells[k] for k in range(1, along)]
    tiles[0] = cells[0]
    tiles[1] = cells[-1]
    for kind, scale in enumerate(KINDS):
        faces = [None] + [(0.5 * scale) * m for m in middles[1:]]
        inverse, lower, ratio, first, last = factor(faces, along)
        for k in range(1, along - 1):
            keep(kind, k, inverse[k], lower[k], ratio[k])
        for k in range(along):
            keep_ends(kind, k, first[k], last[k])
        tiles[2 + kind] = 1.0 + faces[1] * (1.0 - first[1])
        tiles[4 + kind] = faces[1] * last[1]
        tiles[6 + kind] = 1.0 + faces[along - 1] * (1.0 - last[along - 2])


def rolled(value):
    return pltpu.roll(value, 4, 0)


def interface_factor(coef, base, blocks, refs):
    inv_ref, low_ref, rat_ref = refs
    sub = lax.broadcasted_iota(jnp.int32, (8, NZ), 0)
    down = sub < 4
    thermal = (sub == 3) | (sub == 7)

    def row(block, r):
        return jnp.broadcast_to(coef[pl.ds(base(block) + r, 1), :], (8, NZ))

    def by_kind(block, r):
        return jnp.where(thermal, row(block, r + 1), row(block, r))

    scale = jnp.where(thermal, CONDUCT, 1.0).astype(jnp.float32)
    half = blocks // 2
    sides = []
    for i in range(half + 1):
        if i == 0:
            value = jnp.where(down, row(0, 0), row(blocks - 1, 1))
        elif i == half:
            value = 0.5 * (row(i - 1, 1) + row(i, 0))
        else:
            value = 0.5 * jnp.where(
                down,
                row(i - 1, 1) + row(i, 0),
                row(blocks - 1 - i, 1) + row(blocks - i, 0),
            )
        sides.append(scale * value)
    ratio = None
    for i in range(half):
        j = blocks - 1 - i
        couple = jnp.where(down, by_kind(i, 4), by_kind(j, 4))
        even = jnp.where(down, by_kind(i, 2), by_kind(j, 6)) + sides[i]
        odd = jnp.where(down, by_kind(i, 6), by_kind(j, 2)) + sides[i + 1]
        for m, centre, before, after in (
            (2 * i, even, sides[i], couple),
            (2 * i + 1, odd, couple, sides[i + 1]),
        ):
            if m > 0:
                centre = centre - before * ratio
            inverse = 1.0 / centre
            ratio = after * inverse
            inv_ref[m] = inverse
            low_ref[m] = before * inverse
            rat_ref[m] = ratio
    inv_ref[blocks] = 1.0 / (1.0 - ratio * rolled(ratio))


def interface_solve(right, solved, base, blocks, refs):
    inv_ref, low_ref, rat_ref = refs
    down = lax.broadcasted_iota(jnp.int32, (8, NZ), 0) < 4
    half = blocks // 2
    forward = []
    for i in range(half):
        j = blocks - 1 - i
        mine, other = right[pl.ds(base(i), 8), :], right[pl.ds(base(j), 8), :]
        even = jnp.where(down, mine, other)
        odd = rolled(jnp.where(down, other, mine))
        for m, value in ((2 * i, even), (2 * i + 1, odd)):
            value = inv_ref[m] * value
            if m > 0:
                value = value + low_ref[m] * forward[-1]
            forward.append(value)
    tail = forward[-1]
    values = [None] * blocks
    values[-1] = (tail + rat_ref[blocks - 1] * rolled(tail)) * inv_ref[blocks]
    for m in range(blocks - 2, -1, -1):
        values[m] = forward[m] + rat_ref[m] * values[m + 1]
    for i in range(half):
        j = blocks - 1 - i
        even, odd = values[2 * i], rolled(values[2 * i + 1])
        solved[pl.ds(base(i), 8), :] = jnp.where(down, even, odd)
        solved[pl.ds(base(j), 8), :] = jnp.where(down, odd, even)


def far_first(size_a, size_b):
    hops = lambda d, size: min(d, size - d)
    offsets = [(a, b) for a in range(size_a) for b in range(size_b)]
    return sorted(offsets, key=lambda o: -hops(o[0], size_a) - hops(o[1], size_b))


def kernel(flow, visc, inner_y, first_y, last_y, yg, flat, vbuf, cur, inner, part, *rest):
    inv_x, low_x, rat_x, first_x, last_x = rest[0:5]
    inv_y, low_y, rat_y = rest[5:8]
    xi, yi = rest[8:11], rest[11:14]
    cxs, cxr, cys, cyr, xs, xr, xb, xg, ys, yr, yb = rest[14:25]
    xh_low, xh_high, yh_low, yh_high = rest[25:29]
    in_sem, send_sem, recv_sem, halo_send, halo_recv, meet = rest[29:]
    gx, gy = lax.axis_index("gx"), lax.axis_index("gy")

    barrier = pltpu.get_barrier_semaphore()
    ring_z, cores = 8, 2
    ring_x, ring_y = PX // ring_z, PY // cores
    cx, cz = lax.div(gx, ring_z), lax.rem(gx, ring_z)
    cy, cc = lax.div(gy, cores), lax.rem(gy, cores)
    other = cy * cores + 1 - cc
    piece = LX * 8 // ring_y

    def on_x(dx, dz):
        return lax.rem(cx + dx, ring_x) * ring_z + lax.rem(cz + dz, ring_z)

    x_peers = [on_x(dx, dz) for dx, dz in far_first(ring_x, ring_z)]
    y_peers = [lax.rem(cy + dy, ring_y) for dy, _ in far_first(ring_y, 1)]
    column = [(on_x(dx, 0), gy) for dx, _ in far_first(ring_x, 1)[:-1]]
    up, down = (lax.rem(gx + 1, PX), gy), (lax.rem(gx + PX - 1, PX), gy)
    right, left = (gx, lax.rem(gy + 1, PY)), (gx, lax.rem(gy + PY - 1, PY))
    known = [(on_x(0, dz), other) for _, dz in far_first(1, ring_z)] + column + [up, down]
    known += [(gx, chip * cores + core) for chip in y_peers[:-1] for core in range(cores)]

    def greet(sem, devices):
        for device in devices:
            pl.semaphore_signal(sem, inc=1, device_id=device, device_id_type=MESH)

    greet(barrier, known)

    visc_in = pltpu.make_async_copy(visc, vbuf, in_sem.at[0])
    visc_in.start()
    wide = LY + 16

    def cells(k, shift=0):
        return pl.ds((k + 1) * wide + Y0 + shift, LY)

    flow_in = [
        pltpu.make_async_copy(flow.at[:, k], flat.at[:, cells(k), :], in_sem.at[1 + k])
        for k in range(LX)
    ]
    for copy in flow_in:
        copy.start()

    slab, edge = jnp.zeros((LY, NZ), jnp.float32), jnp.zeros((LX, NZ), jnp.float32)
    for f in range(NF):
        flat[f, cells(-1), :] = slab
        flat[f, cells(LX), :] = slab
        flat[f, pl.ds(wide + Y0 - 1, LX, stride=wide), :] = edge
        flat[f, pl.ds(wide + Y0 + LY, LX, stride=wide), :] = edge
        inner[f, pl.ds(0, LY), :] = slab
        inner[f, pl.ds((LX - 1) * LY, LY), :] = slab
        inner_y[f, pl.ds(0, LX, stride=LY), :] = edge
        inner_y[f, pl.ds(LY - 1, LX, stride=LY), :] = edge

    has_up, has_down = gx < PX - 1, gx > 0
    has_right, has_left = gy < PY - 1, gy > 0

    @pl.when(gx == 0)
    def _():
        xh_low[...] = jnp.zeros_like(xh_low)

    @pl.when(gx == PX - 1)
    def _():
        xh_high[...] = jnp.zeros_like(xh_high)

    @pl.when(gy == 0)
    def _():
        yh_low[...] = jnp.zeros_like(yh_low)

    @pl.when(gy == PY - 1)
    def _():
        yh_high[...] = jnp.zeros_like(yh_high)

    def x_rows(k):
        return pl.ds(pl.multiple_of(k * LY, 8), LY)

    def y_rows(k):
        return pl.ds(k, LX, stride=LY)

    def keep_x(kind, k, inverse, lower, ratio):
        inv_x[kind, x_rows(k), :] = inverse
        low_x[kind, x_rows(k), :] = lower
        rat_x[kind, x_rows(k), :] = ratio

    def keep_x_ends(kind, k, first, last):
        first_x[kind, x_rows(k), :] = first
        last_x[kind, x_rows(k), :] = last

    def keep_y(kind, k, inverse, lower, ratio):
        inv_y[kind, pl.ds(k * LX, LX), :] = inverse
        low_y[kind, pl.ds(k * LX, LX), :] = lower
        rat_y[kind, pl.ds(k * LX, LX), :] = ratio

    def keep_y_ends(kind, k, first, last):
        first_y[kind, y_rows(k), :] = first
        last_y[kind, y_rows(k), :] = last

    visc_in.wait()
    tiles = {}
    keep_factor(lambda k: vbuf[x_rows(k), :], LX, keep_x, keep_x_ends, tiles)
    for r in range(8):
        cxs[pl.ds(r, LY, stride=8), :] = tiles[r]

    for copy in flow_in:
        copy.wait()
    pl.semaphore_wait(barrier, len(known))
    greet(meet, column)

    def halo(n, src, dst, device):
        return pltpu.make_async_remote_copy(
            src_ref=src,
            dst_ref=dst,
            send_sem=halo_send.at[n],
            recv_sem=halo_recv.at[n],
            device_id=device,
            device_id_type=MESH,
        )

    x_up = halo(0, flat.at[:, cells(LX - 1), :], xh_low, up)
    x_down = halo(1, flat.at[:, cells(0), :], xh_high, down)
    y_up = halo(2, flow.at[:, :, LY - 1, :], yh_low, right)
    y_down = halo(3, flow.at[:, :, 0, :], yh_high, left)
    pl.when(has_up)(x_up.start)
    pl.when(has_down)(x_down.start)
    pl.when(has_right)(y_up.start)
    pl.when(has_left)(y_down.start)

    def send(src, there, dst, here, size, n, device):
        return pltpu.make_async_remote_copy(
            src_ref=src.at[pl.ds(pl.multiple_of(there * size, 8), size), :],
            dst_ref=dst.at[pl.ds(pl.multiple_of(here * size, 8), size), :],
            send_sem=send_sem.at[n],
            recv_sem=recv_sem.at[n],
            device_id=device,
            device_id_type=MESH,
        )

    def spread_x(src, dst, n):
        for peer in x_peers:
            send(src, peer, dst, gx, 8, n, (peer, other)).start()

    def gather_y(src, dst, n):
        for chip in y_peers[:-1]:
            send(src, chip, dst, gy, piece, n, (gx, chip * cores + 1)).start()
        near = send(src, cy, dst, gy, piece, n, (gx, other))
        pl.when(cc == 0)(near.start)

        @pl.when(cc == 1)
        def _():
            dst[pl.ds(pl.multiple_of(gy * piece, 8), piece), :] = src[
                pl.ds(pl.multiple_of(cy * piece, 8), piece), :
            ]

    def spread_y(src, dst, n):
        for chip in y_peers[:-1]:
            for core in range(cores):
                peer = chip * cores + core
                send(src, peer, dst, cy, piece, n, (gx, peer)).start()
        send(src, other, dst, cy, piece, n, (gx, other)).start()
        dst[pl.ds(pl.multiple_of(cy * piece, 8), piece), :] = src[
            pl.ds(pl.multiple_of(gy * piece, 8), piece), :
        ]

    def take(ref, sem, n, rows):
        part = ref.at[pl.ds(0, rows), :]
        pltpu.make_async_copy(part, part, sem.at[n]).wait()

    def arrived(dst, n, rows):
        take(dst, recv_sem, n, rows)

    def departed(src, n, rows):
        take(src, send_sem, n, rows)

    all_x = 8 * PX
    to_core_1 = (PY - 1) * piece

    def source_row(k, sums):
        here = [flat[f, cells(k), :] for f in range(NF)]
        firsts, lasts = [], []
        for f in range(NF):
            across_x = flat[f, cells(k + 1), :] - flat[f, cells(k - 1), :]
            across_y = flat[f, cells(k, 1), :] - flat[f, cells(k, -1), :]
            across_z = pltpu.roll(here[f], NZ - 1, 1) - pltpu.roll(here[f], 1, 1)
            carried = here[0] * across_x + here[1] * across_y + here[2] * across_z
            source = here[f] - (0.5 * ADVECT) * carried
            if f == 2:
                source = source + BUOYANT * here[3]
            cur[f, x_rows(k), :] = source
            kind = KIND_OF[f]
            firsts.append(sums[f] + first_x[kind, x_rows(k), :] * source)
            lasts.append(sums[NF + f] + last_x[kind, x_rows(k), :] * source)
        return tuple(firsts + lasts)

    sums = (slab,) * (2 * NF)
    for k in range(LX):
        sums = source_row(k, sums)
    for r in range(8):
        xs[pl.ds(r, LY, stride=8), :] = sums[r]

    pl.semaphore_wait(meet, len(column))
    spread_x(cxs, cxr, 0)
    tiles = {}
    keep_factor(lambda k: vbuf[y_rows(k), :], LY, keep_y, keep_y_ends, tiles)
    for r in range(8):
        cys[pl.ds(r, LX, stride=8), :] = tiles[r]
    gather_y(cys, cyr, 1)

    half = 0.5 * ADVECT
    pl.when(has_left)(y_up.wait_recv)
    pl.when(has_right)(y_down.wait_recv)
    for at, around, sign in ((0, yh_low, half), (LY - 1, yh_high, -half)):
        speed = sign * flat[1, pl.ds(wide + Y0 + at, LX, stride=wide), :]
        for f in range(NF):
            kind = KIND_OF[f]
            change = speed * around[f]
            cur[f, y_rows(at), :] = cur[f, y_rows(at), :] + change
            for r, weight in ((f, first_x), (NF + f, last_x)):
                row = pl.ds(at * 8 + r, 1)
                total = jnp.sum(weight[kind, y_rows(at), :] * change, axis=0, keepdims=True)
                xs[row, :] = xs[row, :] + total
    pl.when(has_down)(x_up.wait_recv)
    pl.when(has_up)(x_down.wait_recv)
    for r, at, around, sign in ((0, 0, xh_low, half), (NF, LX - 1, xh_high, -half)):
        speed = sign * flat[0, cells(at), :]
        for f in range(NF):
            row = pl.ds(r + f, LY, stride=8)
            xs[row, :] = xs[row, :] + speed * around[f]
    spread_x(xs, xr, 2)

    def x_down_row(k, before):
        result = []
        for f in range(NF):
            kind = KIND_OF[f]
            value = inv_x[kind, x_rows(k), :] * cur[f, x_rows(k), :] + low_x[kind, x_rows(k), :] * before[f]
            inner[f, x_rows(k), :] = value
            result.append(value)
        return tuple(result)

    def x_up_row(step, after):
        k = LX - 3 - step
        result = []
        for f in range(NF):
            value = inner[f, x_rows(k), :] + rat_x[KIND_OF[f], x_rows(k), :] * after[f]
            inner[f, x_rows(k), :] = value
            result.append(value)
        return tuple(result)

    tail = lax.fori_loop(1, LX - 1, x_down_row, (slab,) * NF)
    lax.fori_loop(0, LX - 3, x_up_row, tail)

    arrived(cxr, 0, all_x)
    interface_factor(cxr, lambda b: 8 * b, PX, xi)
    arrived(xr, 2, all_x)
    interface_solve(xr, xb, lambda b: 8 * b, PX, xi)
    spread_x(xb, xg, 3)

    @pl.when(cc == 1)
    def _():
        arrived(cyr, 1, to_core_1)
        for t in range(piece // 8):
            base = lambda b, t=t: piece * b + 8 * t
            interface_factor(cyr, base, PY, [ref.at[t] for ref in yi])

    arrived(xg, 3, all_x)

    for f in range(NF):
        kind = KIND_OF[f]
        start, end = xg[pl.ds(f, LY, stride=8), :], xg[pl.ds(NF + f, LY, stride=8), :]

        def x_row(k, carry, f=f, kind=kind, start=start, end=end):
            rows = x_rows(k)
            value = inner[f, rows, :] + first_x[kind, rows, :] * start + last_x[kind, rows, :] * end
            cur[f, rows, :] = value
            for r, weight in ((f, first_y), (NF + f, last_y)):
                share = weight[kind, rows, :] * value
                total = share[0:8]
                for q in range(8, LY, 8):
                    total = total + share[q : q + 8]
                part[pl.ds(pl.multiple_of(k * 64, 8) + 8 * r, 8), :] = total
            return carry

        lax.fori_loop(0, LX, x_row, 0, unroll=4)
    for k in range(LX):
        total = part[pl.ds(64 * k, 8, stride=8), :]
        for q in range(1, 8):
            total = total + part[pl.ds(64 * k + q, 8, stride=8), :]
        ys[pl.ds(8 * k, 8), :] = total
    gather_y(ys, yr, 4)

    before = [edge] * NF
    for k in range(1, LY - 1):
        rows = pl.ds(k * LX, LX)
        for f in range(NF):
            kind = KIND_OF[f]
            before[f] = inv_y[kind, rows, :] * cur[f, y_rows(k), :] + low_y[kind, rows, :] * before[f]
            inner[f, rows, :] = before[f]
    after = before
    for f in range(NF):
        inner_y[f, y_rows(LY - 2), :] = after[f]
    for k in range(LY - 3, 0, -1):
        rows = pl.ds(k * LX, LX)
        for f in range(NF):
            after[f] = inner[f, rows, :] + rat_y[KIND_OF[f], rows, :] * after[f]
            inner_y[f, y_rows(k), :] = after[f]

    @pl.when(cc == 1)
    def _():
        arrived(yr, 4, to_core_1)
        for t in range(piece // 8):
            base = lambda b, t=t: piece * b + 8 * t
            interface_solve(yr, yb, base, PY, [ref.at[t] for ref in yi])
        spread_y(yb, yg, 5)

    pl.when(has_up)(x_up.wait_send)
    pl.when(has_down)(x_down.wait_send)
    pl.when(has_right)(y_up.wait_send)
    pl.when(has_left)(y_down.wait_send)
    departed(cxs, 0, all_x)
    departed(xs, 2, all_x)
    departed(xb, 3, all_x)

    @pl.when(cc == 0)
    def _():
        departed(cys, 1, ring_y * piece)
        departed(ys, 4, ring_y * piece)
        arrived(yg, 5, ring_y * piece)

    @pl.when(cc == 1)
    def _():
        if ring_y > 1:
            departed(cys, 1, (ring_y - 1) * piece)
            departed(ys, 4, (ring_y - 1) * piece)
            arrived(yg, 5, (ring_y - 1) * piece)
        departed(yb, 5, to_core_1)


CHUNK = 4


def assemble(inner, first, last, ends, out, done, sem):
    copies = []
    for k in range(LX):
        rows = pl.ds(k * LY, LY)
        for f in range(NF):
            kind = KIND_OF[f]
            done[f, rows, :] = (
                inner[f, rows, :]
                + first[kind, rows, :] * ends[pl.ds(8 * k + f, 1), :]
                + last[kind, rows, :] * ends[pl.ds(8 * k + NF + f, 1), :]
            )
        if k % CHUNK == CHUNK - 1:
            rows = pl.ds((k + 1 - CHUNK) * LY, CHUNK * LY)
            copies.append(
                pltpu.make_async_copy(done.at[:, rows, :], out.at[:, rows, :], sem.at[k // CHUNK])
            )
            copies[-1].start()
    for copy in copies:
        copy.wait()


def per_device(flow_state, viscosity):
    f32 = jnp.float32
    vmem = lambda *shape: pltpu.VMEM(shape, f32)
    rows = LX * LY
    in_vmem = pl.BlockSpec(memory_space=pltpu.VMEM)
    kept = pl.pallas_call(
        kernel,
        out_shape=[
            vmem(NF, rows, NZ),
            vmem(2, rows, NZ),
            vmem(2, rows, NZ),
            vmem(8 * LX, NZ),
        ],
        in_specs=[pl.BlockSpec(memory_space=pl.ANY)] * 2,
        out_specs=[in_vmem] * 4,
        scratch_shapes=[
            vmem(NF, (LX + 2) * (LY + 16), NZ),
            vmem(rows, NZ),
            vmem(NF, rows, NZ),
            vmem(NF, rows, NZ),
            vmem(LX * 64, NZ),
            *[vmem(2, rows, NZ)] * 8,
            *[vmem(PX + 1, 8, NZ)] * 3,
            *[vmem(8, PY + 1, 8, NZ)] * 3,
            *[vmem(8 * PX, NZ)] * 2,
            vmem(8 * LX, NZ),
            vmem(16 * LX, NZ),
            *[vmem(8 * PX, NZ)] * 4,
            vmem(8 * LX, NZ),
            *[vmem(16 * LX, NZ)] * 2,
            *[vmem(NF, LY, NZ)] * 2,
            *[vmem(NF, LX, NZ)] * 2,
            pltpu.SemaphoreType.DMA((1 + LX,)),
            pltpu.SemaphoreType.DMA((6,)),
            pltpu.SemaphoreType.DMA((6,)),
            pltpu.SemaphoreType.DMA((4,)),
            pltpu.SemaphoreType.DMA((4,)),
            pltpu.SemaphoreType.REGULAR,
        ],
        compiler_params=pltpu.CompilerParams(collective_id=0, has_side_effects=True),
    )(flow_state, viscosity.reshape(rows, NZ))
    result = pl.pallas_call(
        assemble,
        out_shape=jax.ShapeDtypeStruct((NF, rows, NZ), f32),
        in_specs=[in_vmem] * 4,
        out_specs=pl.BlockSpec(memory_space=pl.ANY),
        scratch_shapes=[vmem(NF, rows, NZ), pltpu.SemaphoreType.DMA((LX // CHUNK,))],
        compiler_params=pltpu.CompilerParams(vmem_limit_bytes=8 << 20),
    )(*kept)
    return result.reshape(NF, LX, LY, NZ)


def solution(mesh):
    return jax.shard_map(
        per_device,
        mesh=mesh,
        in_specs=(P(None, "gx", "gy", None), P("gx", "gy", None)),
        out_specs=P(None, "gx", "gy", None),
        check_vma=False,
    )
```

```python
import jax
import jax.numpy as jnp
from jax import lax
from jax.experimental import pallas as pl
from jax.experimental.pallas import tpu as pltpu
from jax.sharding import PartitionSpec as P

MESH = pl.DeviceIdType.MESH

ADVECT = 0.2
BUOYANT = 0.5
CONDUCT = 0.6
KINDS = (1.0, CONDUCT)
KIND_OF = (0, 0, 0, 1)

NF = 4
LX, LY, NZ = 16, 32, 128
PX, PY = 32, 8
Y0 = 8


def factor(faces, along):
    inverse, lower, ratio = {}, {}, {}
    one = jnp.ones_like(faces[1])
    running = one
    forward = {}
    for k in range(1, along - 1):
        centre = 1.0 + faces[k] + faces[k + 1]
        if k > 1:
            centre = centre - faces[k] * ratio[k - 1]
        inverse[k] = 1.0 / centre
        lower[k] = faces[k] * inverse[k]
        ratio[k] = faces[k + 1] * inverse[k]
        running = lower[k] * running
        forward[k] = running
    first, last = {along - 1: jnp.zeros_like(one)}, {along - 1: one}
    for k in range(along - 2, 0, -1):
        first[k] = forward[k] + ratio[k] * first[k + 1]
        last[k] = ratio[k] * last[k + 1]
    first[0], last[0] = one, jnp.zeros_like(one)
    return inverse, lower, ratio, first, last


def keep_factor(load, along, keep, keep_ends, tiles):
    cells = [load(k) for k in range(along)]
    middles = [None] + [cells[k - 1] + cells[k] for k in range(1, along)]
    tiles[0] = cells[0]
    tiles[1] = cells[-1]
    for kind, scale in enumerate(KINDS):
        faces = [None] + [(0.5 * scale) * m for m in middles[1:]]
        inverse, lower, ratio, first, last = factor(faces, along)
        for k in range(1, along - 1):
            keep(kind, k, inverse[k], lower[k], ratio[k])
        for k in range(along):
            keep_ends(kind, k, first[k], last[k])
        tiles[2 + kind] = 1.0 + faces[1] * (1.0 - first[1])
        tiles[4 + kind] = faces[1] * last[1]
        tiles[6 + kind] = 1.0 + faces[along - 1] * (1.0 - last[along - 2])


def rolled(value):
    return pltpu.roll(value, 4, 0)


def interface_factor(coef, base, blocks, refs):
    inv_ref, low_ref, rat_ref = refs
    sub = lax.broadcasted_iota(jnp.int32, (8, NZ), 0)
    down = sub < 4
    thermal = (sub == 3) | (sub == 7)

    def row(block, r):
        return jnp.broadcast_to(coef[pl.ds(base(block) + r, 1), :], (8, NZ))

    def by_kind(block, r):
        return jnp.where(thermal, row(block, r + 1), row(block, r))

    scale = jnp.where(thermal, CONDUCT, 1.0).astype(jnp.float32)
    half = blocks // 2
    sides = []
    for i in range(half + 1):
        if i == 0:
            value = jnp.where(down, row(0, 0), row(blocks - 1, 1))
        elif i == half:
            value = 0.5 * (row(i - 1, 1) + row(i, 0))
        else:
            value = 0.5 * jnp.where(
                down,
                row(i - 1, 1) + row(i, 0),
                row(blocks - 1 - i, 1) + row(blocks - i, 0),
            )
        sides.append(scale * value)
    ratio = None
    for i in range(half):
        j = blocks - 1 - i
        couple = jnp.where(down, by_kind(i, 4), by_kind(j, 4))
        even = jnp.where(down, by_kind(i, 2), by_kind(j, 6)) + sides[i]
        odd = jnp.where(down, by_kind(i, 6), by_kind(j, 2)) + sides[i + 1]
        for m, centre, before, after in (
            (2 * i, even, sides[i], couple),
            (2 * i + 1, odd, couple, sides[i + 1]),
        ):
            if m > 0:
                centre = centre - before * ratio
            inverse = 1.0 / centre
            ratio = after * inverse
            inv_ref[m] = inverse
            low_ref[m] = before * inverse
            rat_ref[m] = ratio
    inv_ref[blocks] = 1.0 / (1.0 - ratio * rolled(ratio))


def interface_solve(right, solved, base, blocks, refs):
    inv_ref, low_ref, rat_ref = refs
    down = lax.broadcasted_iota(jnp.int32, (8, NZ), 0) < 4
    half = blocks // 2
    forward = []
    for i in range(half):
        j = blocks - 1 - i
        mine, other = right[pl.ds(base(i), 8), :], right[pl.ds(base(j), 8), :]
        even = jnp.where(down, mine, other)
        odd = rolled(jnp.where(down, other, mine))
        for m, value in ((2 * i, even), (2 * i + 1, odd)):
            value = inv_ref[m] * value
            if m > 0:
                value = value + low_ref[m] * forward[-1]
            forward.append(value)
    tail = forward[-1]
    values = [None] * blocks
    values[-1] = (tail + rat_ref[blocks - 1] * rolled(tail)) * inv_ref[blocks]
    for m in range(blocks - 2, -1, -1):
        values[m] = forward[m] + rat_ref[m] * values[m + 1]
    for i in range(half):
        j = blocks - 1 - i
        even, odd = values[2 * i], rolled(values[2 * i + 1])
        solved[pl.ds(base(i), 8), :] = jnp.where(down, even, odd)
        solved[pl.ds(base(j), 8), :] = jnp.where(down, odd, even)


def far_first(size_a, size_b):
    hops = lambda d, size: min(d, size - d)
    offsets = [(a, b) for a in range(size_a) for b in range(size_b)]
    return sorted(offsets, key=lambda o: -hops(o[0], size_a) - hops(o[1], size_b))


def kernel(flow, visc, inner_y, first_y, last_y, yg, flat, vbuf, cur, inner, part, *rest):
    inv_x, low_x, rat_x, first_x, last_x = rest[0:5]
    inv_y, low_y, rat_y = rest[5:8]
    xi, yi = rest[8:11], rest[11:14]
    cxs, cxr, cys, cyr, xs, xr, xb, xg, ys, yr, yb = rest[14:25]
    xh_low, xh_high, yh_low, yh_high = rest[25:29]
    in_sem, send_sem, recv_sem, halo_send, halo_recv, meet = rest[29:]
    gx, gy = lax.axis_index("gx"), lax.axis_index("gy")

    barrier = pltpu.get_barrier_semaphore()
    ring_z, cores = 8, 2
    ring_x, ring_y = PX // ring_z, PY // cores
    cx, cz = lax.div(gx, ring_z), lax.rem(gx, ring_z)
    cy, cc = lax.div(gy, cores), lax.rem(gy, cores)
    other = cy * cores + 1 - cc
    piece = LX * 8 // ring_y

    def on_x(dx, dz):
        return lax.rem(cx + dx, ring_x) * ring_z + lax.rem(cz + dz, ring_z)

    x_peers = [on_x(dx, dz) for dx, dz in far_first(ring_x, ring_z)]
    y_peers = [lax.rem(cy + dy, ring_y) for dy, _ in far_first(ring_y, 1)]
    column = [(on_x(dx, 0), gy) for dx, _ in far_first(ring_x, 1)[:-1]]
    up, down = (lax.rem(gx + 1, PX), gy), (lax.rem(gx + PX - 1, PX), gy)
    right, left = (gx, lax.rem(gy + 1, PY)), (gx, lax.rem(gy + PY - 1, PY))
    known = [(on_x(0, dz), other) for _, dz in far_first(1, ring_z)] + column + [up, down]
    known += [(gx, chip * cores + core) for chip in y_peers[:-1] for core in range(cores)]

    def greet(sem, devices):
        for device in devices:
            pl.semaphore_signal(sem, inc=1, device_id=device, device_id_type=MESH)

    greet(barrier, known)

    visc_in = pltpu.make_async_copy(visc, vbuf, in_sem.at[0])
    visc_in.start()
    wide = LY + 16

    def cells(k, shift=0):
        return pl.ds((k + 1) * wide + Y0 + shift, LY)

    flow_in = [
        pltpu.make_async_copy(flow.at[:, k], flat.at[:, cells(k), :], in_sem.at[1 + k])
        for k in range(LX)
    ]
    for copy in flow_in:
        copy.start()

    slab, edge = jnp.zeros((LY, NZ), jnp.float32), jnp.zeros((LX, NZ), jnp.float32)
    for f in range(NF):
        flat[f, cells(-1), :] = slab
        flat[f, cells(LX), :] = slab
        flat[f, pl.ds(wide + Y0 - 1, LX, stride=wide), :] = edge
        flat[f, pl.ds(wide + Y0 + LY, LX, stride=wide), :] = edge
        inner[f, pl.ds(0, LY), :] = slab
        inner[f, pl.ds((LX - 1) * LY, LY), :] = slab
        inner_y[f, pl.ds(0, LX, stride=LY), :] = edge
        inner_y[f, pl.ds(LY - 1, LX, stride=LY), :] = edge

    has_up, has_down = gx < PX - 1, gx > 0
    has_right, has_left = gy < PY - 1, gy > 0

    @pl.when(gx == 0)
    def _():
        xh_low[...] = jnp.zeros_like(xh_low)

    @pl.when(gx == PX - 1)
    def _():
        xh_high[...] = jnp.zeros_like(xh_high)

    @pl.when(gy == 0)
    def _():
        yh_low[...] = jnp.zeros_like(yh_low)

    @pl.when(gy == PY - 1)
    def _():
        yh_high[...] = jnp.zeros_like(yh_high)

    def x_rows(k):
        return pl.ds(pl.multiple_of(k * LY, 8), LY)

    def y_rows(k):
        return pl.ds(k, LX, stride=LY)

    def keep_x(kind, k, inverse, lower, ratio):
        inv_x[kind, x_rows(k), :] = inverse
        low_x[kind, x_rows(k), :] = lower
        rat_x[kind, x_rows(k), :] = ratio

    def keep_x_ends(kind, k, first, last):
        first_x[kind, x_rows(k), :] = first
        last_x[kind, x_rows(k), :] = last

    def keep_y(kind, k, inverse, lower, ratio):
        inv_y[kind, pl.ds(k * LX, LX), :] = inverse
        low_y[kind, pl.ds(k * LX, LX), :] = lower
        rat_y[kind, pl.ds(k * LX, LX), :] = ratio

    def keep_y_ends(kind, k, first, last):
        first_y[kind, y_rows(k), :] = first
        last_y[kind, y_rows(k), :] = last

    visc_in.wait()
    tiles = {}
    keep_factor(lambda k: vbuf[x_rows(k), :], LX, keep_x, keep_x_ends, tiles)
    for r in range(8):
        cxs[pl.ds(r, LY, stride=8), :] = tiles[r]

    for copy in flow_in:
        copy.wait()
    pl.semaphore_wait(barrier, len(known))
    greet(meet, column)

    def halo(n, src, dst, device):
        return pltpu.make_async_remote_copy(
            src_ref=src,
            dst_ref=dst,
            send_sem=halo_send.at[n],
            recv_sem=halo_recv.at[n],
            device_id=device,
            device_id_type=MESH,
        )

    strip = LY // ring_x
    row_order = [dx for dx, _ in far_first(ring_x, 1)]

    def strip_at(n, device_x):
        return pl.multiple_of(lax.rem(device_x + row_order[n], ring_x) * strip, 8)

    def x_halo(n, toward, k, dst):
        at = strip_at(n % ring_x, lax.div(toward[0], ring_z))
        src = flat.at[:, pl.ds((k + 1) * wide + Y0 + at, strip), :]
        return halo(n, src, dst.at[:, pl.ds(at, strip), :], toward)

    x_up = [x_halo(n, up, LX - 1, xh_low) for n in range(ring_x)]
    x_down = [x_halo(ring_x + n, down, 0, xh_high) for n in range(ring_x)]
    y_up = halo(2 * ring_x, flow.at[:, :, LY - 1, :], yh_low, right)
    y_down = halo(2 * ring_x + 1, flow.at[:, :, 0, :], yh_high, left)
    pl.when(has_right)(y_up.start)
    pl.when(has_left)(y_down.start)
    for n in range(ring_x):
        pl.when(has_up)(x_up[n].start)
        pl.when(has_down)(x_down[n].start)

    def send(src, there, dst, here, size, n, device, arrival=None):
        return pltpu.make_async_remote_copy(
            src_ref=src.at[pl.ds(pl.multiple_of(there * size, 8), size), :],
            dst_ref=dst.at[pl.ds(pl.multiple_of(here * size, 8), size), :],
            send_sem=send_sem.at[n],
            recv_sem=recv_sem.at[n if arrival is None else arrival],
            device_id=device,
            device_id_type=MESH,
        )

    def spread_x(src, dst, n):
        for peer in x_peers:
            send(src, peer, dst, gx, 8, n, (peer, other)).start()

    def gather_y(src, dst, n):
        for chip in y_peers[:-1]:
            send(src, chip, dst, gy, piece, n, (gx, chip * cores + 1)).start()
        near = send(src, cy, dst, gy, piece, n, (gx, other))
        pl.when(cc == 0)(near.start)

        @pl.when(cc == 1)
        def _():
            dst[pl.ds(pl.multiple_of(gy * piece, 8), piece), :] = src[
                pl.ds(pl.multiple_of(cy * piece, 8), piece), :
            ]

    def spread_y(src, dst, n):
        for chip in y_peers[:-1]:
            for core in range(cores):
                peer = chip * cores + core
                send(src, peer, dst, cy, piece, n, (gx, peer)).start()
        send(src, other, dst, cy, piece, n, (gx, other)).start()
        dst[pl.ds(pl.multiple_of(cy * piece, 8), piece), :] = src[
            pl.ds(pl.multiple_of(gy * piece, 8), piece), :
        ]

    def take(ref, sem, n, rows):
        part = ref.at[pl.ds(0, rows), :]
        pltpu.make_async_copy(part, part, sem.at[n]).wait()

    def arrived(dst, n, rows):
        take(dst, recv_sem, n, rows)

    def departed(src, n, rows):
        take(src, send_sem, n, rows)

    all_x = 8 * PX
    to_core_1 = (PY - 1) * piece

    def source_row(k, sums):
        here = [flat[f, cells(k), :] for f in range(NF)]
        firsts, lasts = [], []
        for f in range(NF):
            across_x = flat[f, cells(k + 1), :] - flat[f, cells(k - 1), :]
            across_y = flat[f, cells(k, 1), :] - flat[f, cells(k, -1), :]
            across_z = pltpu.roll(here[f], NZ - 1, 1) - pltpu.roll(here[f], 1, 1)
            carried = here[0] * across_x + here[1] * across_y + here[2] * across_z
            source = here[f] - (0.5 * ADVECT) * carried
            if f == 2:
                source = source + BUOYANT * here[3]
            cur[f, x_rows(k), :] = source
            kind = KIND_OF[f]
            firsts.append(sums[f] + first_x[kind, x_rows(k), :] * source)
            lasts.append(sums[NF + f] + last_x[kind, x_rows(k), :] * source)
        return tuple(firsts + lasts)

    sums = (slab,) * (2 * NF)
    for k in range(LX):
        sums = source_row(k, sums)
    for r in range(8):
        xs[pl.ds(r, LY, stride=8), :] = sums[r]

    pl.semaphore_wait(meet, len(column))
    spread_x(cxs, cxr, 0)

    half = 0.5 * ADVECT
    pl.when(has_left)(y_up.wait_recv)
    pl.when(has_right)(y_down.wait_recv)
    for at, around, sign in ((0, yh_low, half), (LY - 1, yh_high, -half)):
        speed = sign * flat[1, pl.ds(wide + Y0 + at, LX, stride=wide), :]
        for f in range(NF):
            kind = KIND_OF[f]
            change = speed * around[f]
            cur[f, y_rows(at), :] = cur[f, y_rows(at), :] + change
            for r, weight in ((f, first_x), (NF + f, last_x)):
                row = pl.ds(at * 8 + r, 1)
                total = jnp.sum(weight[kind, y_rows(at), :] * change, axis=0, keepdims=True)
                xs[row, :] = xs[row, :] + total
    for n in range(ring_x):
        at = strip_at(n, cx)
        pl.when(has_down)(x_up[n].wait_recv)
        pl.when(has_up)(x_down[n].wait_recv)
        for r, edge_k, around, sign in ((0, 0, xh_low, half), (NF, LX - 1, xh_high, -half)):
            speed = sign * flat[0, pl.ds((edge_k + 1) * wide + Y0 + at, strip), :]
            for f in range(NF):
                row = pl.ds(8 * at + r + f, strip, stride=8)
                xs[row, :] = xs[row, :] + speed * around[f, pl.ds(at, strip), :]
        for _, dz in far_first(1, ring_z):
            peer = on_x(row_order[n], dz)
            send(xs, peer, xr, gx, 8, 2, (peer, other)).start()

    def x_down_row(k, before):
        result = []
        for f in range(NF):
            kind = KIND_OF[f]
            value = inv_x[kind, x_rows(k), :] * cur[f, x_rows(k), :] + low_x[kind, x_rows(k), :] * before[f]
            inner[f, x_rows(k), :] = value
            result.append(value)
        return tuple(result)

    def x_up_row(step, after):
        k = LX - 3 - step
        result = []
        for f in range(NF):
            value = inner[f, x_rows(k), :] + rat_x[KIND_OF[f], x_rows(k), :] * after[f]
            inner[f, x_rows(k), :] = value
            result.append(value)
        return tuple(result)

    tail = lax.fori_loop(1, LX - 1, x_down_row, (slab,) * NF)
    lax.fori_loop(0, LX - 3, x_up_row, tail)

    tiles = {}
    keep_factor(lambda k: vbuf[y_rows(k), :], LY, keep_y, keep_y_ends, tiles)
    for r in range(8):
        cys[pl.ds(r, LX, stride=8), :] = tiles[r]
    gather_y(cys, cyr, 1)

    arrived(cxr, 0, all_x)
    interface_factor(cxr, lambda b: 8 * b, PX, xi)
    arrived(xr, 2, all_x)
    interface_solve(xr, xb, lambda b: 8 * b, PX, xi)
    for dx, dz in far_first(ring_x, ring_z):
        peer = on_x(dx, dz)
        send(xb, peer, xg, gx, 8, 3, (peer, other), 6 + (ring_x - dx) % ring_x).start()

    @pl.when(cc == 1)
    def _():
        arrived(cyr, 1, to_core_1)
        for t in range(piece // 8):
            base = lambda b, t=t: piece * b + 8 * t
            interface_factor(cyr, base, PY, [ref.at[t] for ref in yi])

    for n in range(ring_x):
        dx = row_order[ring_x - 1 - n]
        at = pl.multiple_of(lax.rem(cx + dx, ring_x) * strip, 8)
        arrived(xg, 6 + dx, 8 * strip)
        starts = [xg[pl.ds(8 * at + f, strip, stride=8), :] for f in range(NF)]
        ends = [xg[pl.ds(8 * at + NF + f, strip, stride=8), :] for f in range(NF)]

        def x_row(k, carry, n=n, at=at, starts=starts, ends=ends):
            rows = pl.ds(pl.multiple_of(k * LY + at, 8), strip)
            shares = pl.multiple_of(k * 64, 8)
            for f in range(NF):
                kind = KIND_OF[f]
                value = (
                    inner[f, rows, :]
                    + first_x[kind, rows, :] * starts[f]
                    + last_x[kind, rows, :] * ends[f]
                )
                cur[f, rows, :] = value
                for r, weight in ((f, first_y), (NF + f, last_y)):
                    share = weight[kind, rows, :] * value
                    here = pl.ds(shares + 8 * r, 8)
                    part[here, :] = share if n == 0 else part[here, :] + share
            return carry

        lax.fori_loop(0, LX, x_row, 0, unroll=4)
    for k in range(LX):
        total = part[pl.ds(64 * k, 8, stride=8), :]
        for q in range(1, 8):
            total = total + part[pl.ds(64 * k + q, 8, stride=8), :]
        ys[pl.ds(8 * k, 8), :] = total
    gather_y(ys, yr, 4)

    before = [edge] * NF
    for k in range(1, LY - 1):
        rows = pl.ds(k * LX, LX)
        for f in range(NF):
            kind = KIND_OF[f]
            before[f] = inv_y[kind, rows, :] * cur[f, y_rows(k), :] + low_y[kind, rows, :] * before[f]
            inner[f, rows, :] = before[f]
    after = before
    for f in range(NF):
        inner_y[f, y_rows(LY - 2), :] = after[f]
    for k in range(LY - 3, 0, -1):
        rows = pl.ds(k * LX, LX)
        for f in range(NF):
            after[f] = inner[f, rows, :] + rat_y[KIND_OF[f], rows, :] * after[f]
            inner_y[f, y_rows(k), :] = after[f]

    @pl.when(cc == 1)
    def _():
        arrived(yr, 4, to_core_1)
        for t in range(piece // 8):
            base = lambda b, t=t: piece * b + 8 * t
            interface_solve(yr, yb, base, PY, [ref.at[t] for ref in yi])
        spread_y(yb, yg, 5)

    for n in range(ring_x):
        pl.when(has_up)(x_up[n].wait_send)
        pl.when(has_down)(x_down[n].wait_send)
    pl.when(has_right)(y_up.wait_send)
    pl.when(has_left)(y_down.wait_send)
    departed(cxs, 0, all_x)
    departed(xs, 2, all_x)
    departed(xb, 3, all_x)

    @pl.when(cc == 0)
    def _():
        departed(cys, 1, ring_y * piece)
        departed(ys, 4, ring_y * piece)
        arrived(yg, 5, ring_y * piece)

    @pl.when(cc == 1)
    def _():
        if ring_y > 1:
            departed(cys, 1, (ring_y - 1) * piece)
            departed(ys, 4, (ring_y - 1) * piece)
            arrived(yg, 5, (ring_y - 1) * piece)
        departed(yb, 5, to_core_1)


CHUNK = 4


def assemble(inner, first, last, ends, out, done, sem):
    copies = []
    for k in range(LX):
        rows = pl.ds(k * LY, LY)
        for f in range(NF):
            kind = KIND_OF[f]
            done[f, rows, :] = (
                inner[f, rows, :]
                + first[kind, rows, :] * ends[pl.ds(8 * k + f, 1), :]
                + last[kind, rows, :] * ends[pl.ds(8 * k + NF + f, 1), :]
            )
        if k % CHUNK == CHUNK - 1:
            rows = pl.ds((k + 1 - CHUNK) * LY, CHUNK * LY)
            copies.append(
                pltpu.make_async_copy(done.at[:, rows, :], out.at[:, rows, :], sem.at[k // CHUNK])
            )
            copies[-1].start()
    for copy in copies:
        copy.wait()


def per_device(flow_state, viscosity):
    f32 = jnp.float32
    vmem = lambda *shape: pltpu.VMEM(shape, f32)
    rows = LX * LY
    in_vmem = pl.BlockSpec(memory_space=pltpu.VMEM)
    kept = pl.pallas_call(
        kernel,
        out_shape=[
            vmem(NF, rows, NZ),
            vmem(2, rows, NZ),
            vmem(2, rows, NZ),
            vmem(8 * LX, NZ),
        ],
        in_specs=[pl.BlockSpec(memory_space=pl.ANY)] * 2,
        out_specs=[in_vmem] * 4,
        scratch_shapes=[
            vmem(NF, (LX + 2) * (LY + 16), NZ),
            vmem(rows, NZ),
            vmem(NF, rows, NZ),
            vmem(NF, rows, NZ),
            vmem(LX * 64, NZ),
            *[vmem(2, rows, NZ)] * 8,
            *[vmem(PX + 1, 8, NZ)] * 3,
            *[vmem(8, PY + 1, 8, NZ)] * 3,
            *[vmem(8 * PX, NZ)] * 2,
            vmem(8 * LX, NZ),
            vmem(16 * LX, NZ),
            *[vmem(8 * PX, NZ)] * 4,
            vmem(8 * LX, NZ),
            *[vmem(16 * LX, NZ)] * 2,
            *[vmem(NF, LY, NZ)] * 2,
            *[vmem(NF, LX, NZ)] * 2,
            pltpu.SemaphoreType.DMA((1 + LX,)),
            pltpu.SemaphoreType.DMA((6,)),
            pltpu.SemaphoreType.DMA((10,)),
            pltpu.SemaphoreType.DMA((10,)),
            pltpu.SemaphoreType.DMA((10,)),
            pltpu.SemaphoreType.REGULAR,
        ],
        compiler_params=pltpu.CompilerParams(collective_id=0, has_side_effects=True),
    )(flow_state, viscosity.reshape(rows, NZ))
    result = pl.pallas_call(
        assemble,
        out_shape=jax.ShapeDtypeStruct((NF, rows, NZ), f32),
        in_specs=[in_vmem] * 4,
        out_specs=pl.BlockSpec(memory_space=pl.ANY),
        scratch_shapes=[vmem(NF, rows, NZ), pltpu.SemaphoreType.DMA((LX // CHUNK,))],
        compiler_params=pltpu.CompilerParams(vmem_limit_bytes=8 << 20),
    )(*kept)
    return result.reshape(NF, LX, LY, NZ)


def solution(mesh):
    return jax.shard_map(
        per_device,
        mesh=mesh,
        in_specs=(P(None, "gx", "gy", None), P("gx", "gy", None)),
        out_specs=P(None, "gx", "gy", None),
        check_vma=False,
    )
```

```python
import jax
import jax.numpy as jnp
from jax import lax
from jax.experimental import pallas as pl
from jax.experimental.pallas import tpu as pltpu
from jax.sharding import PartitionSpec as P

MESH = pl.DeviceIdType.MESH

ADVECT = 0.2
BUOYANT = 0.5
CONDUCT = 0.6
KINDS = (1.0, CONDUCT)
KIND_OF = (0, 0, 0, 1)

NF = 4
LX, LY, NZ = 16, 32, 128
PX, PY = 32, 8
Y0 = 8


def factor(faces, along):
    inverse, lower, ratio = {}, {}, {}
    one = jnp.ones_like(faces[1])
    running = one
    forward = {}
    for k in range(1, along - 1):
        centre = 1.0 + faces[k] + faces[k + 1]
        if k > 1:
            centre = centre - faces[k] * ratio[k - 1]
        inverse[k] = 1.0 / centre
        lower[k] = faces[k] * inverse[k]
        ratio[k] = faces[k + 1] * inverse[k]
        running = lower[k] * running
        forward[k] = running
    first, last = {along - 1: jnp.zeros_like(one)}, {along - 1: one}
    for k in range(along - 2, 0, -1):
        first[k] = forward[k] + ratio[k] * first[k + 1]
        last[k] = ratio[k] * last[k + 1]
    first[0], last[0] = one, jnp.zeros_like(one)
    return inverse, lower, ratio, first, last


def keep_factor(load, along, keep, keep_ends, tiles):
    cells = [load(k) for k in range(along)]
    middles = [None] + [cells[k - 1] + cells[k] for k in range(1, along)]
    tiles[0] = cells[0]
    tiles[1] = cells[-1]
    for kind, scale in enumerate(KINDS):
        faces = [None] + [(0.5 * scale) * m for m in middles[1:]]
        inverse, lower, ratio, first, last = factor(faces, along)
        for k in range(1, along - 1):
            keep(kind, k, inverse[k], lower[k], ratio[k])
        for k in range(along):
            keep_ends(kind, k, first[k], last[k])
        tiles[2 + kind] = 1.0 + faces[1] * (1.0 - first[1])
        tiles[4 + kind] = faces[1] * last[1]
        tiles[6 + kind] = 1.0 + faces[along - 1] * (1.0 - last[along - 2])


def rolled(value):
    return pltpu.roll(value, 4, 0)


def interface_factor(coef, base, blocks, refs):
    inv_ref, low_ref, rat_ref = refs
    sub = lax.broadcasted_iota(jnp.int32, (8, NZ), 0)
    down = sub < 4
    thermal = (sub == 3) | (sub == 7)

    def row(block, r):
        return jnp.broadcast_to(coef[pl.ds(base(block) + r, 1), :], (8, NZ))

    def by_kind(block, r):
        return jnp.where(thermal, row(block, r + 1), row(block, r))

    scale = jnp.where(thermal, CONDUCT, 1.0).astype(jnp.float32)
    half = blocks // 2
    sides = []
    for i in range(half + 1):
        if i == 0:
            value = jnp.where(down, row(0, 0), row(blocks - 1, 1))
        elif i == half:
            value = 0.5 * (row(i - 1, 1) + row(i, 0))
        else:
            value = 0.5 * jnp.where(
                down,
                row(i - 1, 1) + row(i, 0),
                row(blocks - 1 - i, 1) + row(blocks - i, 0),
            )
        sides.append(scale * value)
    ratio = None
    for i in range(half):
        j = blocks - 1 - i
        couple = jnp.where(down, by_kind(i, 4), by_kind(j, 4))
        even = jnp.where(down, by_kind(i, 2), by_kind(j, 6)) + sides[i]
        odd = jnp.where(down, by_kind(i, 6), by_kind(j, 2)) + sides[i + 1]
        for m, centre, before, after in (
            (2 * i, even, sides[i], couple),
            (2 * i + 1, odd, couple, sides[i + 1]),
        ):
            if m > 0:
                centre = centre - before * ratio
            inverse = 1.0 / centre
            ratio = after * inverse
            inv_ref[m] = inverse
            low_ref[m] = before * inverse
            rat_ref[m] = ratio
    inv_ref[blocks] = 1.0 / (1.0 - ratio * rolled(ratio))


def interface_solve(right, solved, base, blocks, refs):
    inv_ref, low_ref, rat_ref = refs
    down = lax.broadcasted_iota(jnp.int32, (8, NZ), 0) < 4
    half = blocks // 2
    forward = []
    for i in range(half):
        j = blocks - 1 - i
        mine, other = right[pl.ds(base(i), 8), :], right[pl.ds(base(j), 8), :]
        even = jnp.where(down, mine, other)
        odd = rolled(jnp.where(down, other, mine))
        for m, value in ((2 * i, even), (2 * i + 1, odd)):
            value = inv_ref[m] * value
            if m > 0:
                value = value + low_ref[m] * forward[-1]
            forward.append(value)
    tail = forward[-1]
    values = [None] * blocks
    values[-1] = (tail + rat_ref[blocks - 1] * rolled(tail)) * inv_ref[blocks]
    for m in range(blocks - 2, -1, -1):
        values[m] = forward[m] + rat_ref[m] * values[m + 1]
    for i in range(half):
        j = blocks - 1 - i
        even, odd = values[2 * i], rolled(values[2 * i + 1])
        solved[pl.ds(base(i), 8), :] = jnp.where(down, even, odd)
        solved[pl.ds(base(j), 8), :] = jnp.where(down, odd, even)


def far_first(size_a, size_b):
    hops = lambda d, size: min(d, size - d)
    offsets = [(a, b) for a in range(size_a) for b in range(size_b)]
    return sorted(offsets, key=lambda o: -hops(o[0], size_a) - hops(o[1], size_b))


def kernel(flow, visc, inner_y, first_y, last_y, yg, flat, vbuf, cur, inner, part, *rest):
    inv_x, low_x, rat_x, first_x, last_x = rest[0:5]
    inv_y, low_y, rat_y = rest[5:8]
    xi, yi = rest[8:11], rest[11:14]
    cxs, cxr, cys, cyr, xs, xr, xb, xg, ys, yr, yb = rest[14:25]
    xh_low, xh_high, yh_low, yh_high = rest[25:29]
    in_sem, send_sem, recv_sem, halo_send, halo_recv, meet = rest[29:]
    gx, gy = lax.axis_index("gx"), lax.axis_index("gy")

    barrier = pltpu.get_barrier_semaphore()
    ring_z, cores = 8, 2
    ring_x, ring_y = PX // ring_z, PY // cores
    cx, cz = lax.div(gx, ring_z), lax.rem(gx, ring_z)
    cy, cc = lax.div(gy, cores), lax.rem(gy, cores)
    other = cy * cores + 1 - cc
    piece = LX * 8 // ring_y

    def on_x(dx, dz):
        return lax.rem(cx + dx, ring_x) * ring_z + lax.rem(cz + dz, ring_z)

    x_peers = [on_x(dx, dz) for dx, dz in far_first(ring_x, ring_z)]
    y_peers = [lax.rem(cy + dy, ring_y) for dy, _ in far_first(ring_y, 1)]
    column = [(on_x(dx, 0), gy) for dx, _ in far_first(ring_x, 1)[:-1]]
    up, down = (lax.rem(gx + 1, PX), gy), (lax.rem(gx + PX - 1, PX), gy)
    right, left = (gx, lax.rem(gy + 1, PY)), (gx, lax.rem(gy + PY - 1, PY))
    known = [(on_x(0, dz), other) for _, dz in far_first(1, ring_z)] + column + [up, down]
    known += [(gx, chip * cores + core) for chip in y_peers[:-1] for core in range(cores)]

    def greet(sem, devices):
        for device in devices:
            pl.semaphore_signal(sem, inc=1, device_id=device, device_id_type=MESH)

    greet(barrier, known)

    visc_in = pltpu.make_async_copy(visc, vbuf, in_sem.at[0])
    visc_in.start()
    wide = LY + 16

    def cells(k, shift=0):
        return pl.ds((k + 1) * wide + Y0 + shift, LY)

    flow_in = [
        pltpu.make_async_copy(flow.at[:, k], flat.at[:, cells(k), :], in_sem.at[1 + k])
        for k in range(LX)
    ]
    for copy in flow_in:
        copy.start()

    slab, edge = jnp.zeros((LY, NZ), jnp.float32), jnp.zeros((LX, NZ), jnp.float32)
    for f in range(NF):
        flat[f, cells(-1), :] = slab
        flat[f, cells(LX), :] = slab
        flat[f, pl.ds(wide + Y0 - 1, LX, stride=wide), :] = edge
        flat[f, pl.ds(wide + Y0 + LY, LX, stride=wide), :] = edge
        inner[f, pl.ds(0, LY), :] = slab
        inner[f, pl.ds((LX - 1) * LY, LY), :] = slab
        inner_y[f, pl.ds(0, LX, stride=LY), :] = edge
        inner_y[f, pl.ds(LY - 1, LX, stride=LY), :] = edge

    has_up, has_down = gx < PX - 1, gx > 0
    has_right, has_left = gy < PY - 1, gy > 0

    @pl.when(gx == 0)
    def _():
        xh_low[...] = jnp.zeros_like(xh_low)

    @pl.when(gx == PX - 1)
    def _():
        xh_high[...] = jnp.zeros_like(xh_high)

    @pl.when(gy == 0)
    def _():
        yh_low[...] = jnp.zeros_like(yh_low)

    @pl.when(gy == PY - 1)
    def _():
        yh_high[...] = jnp.zeros_like(yh_high)

    def x_rows(k):
        return pl.ds(pl.multiple_of(k * LY, 8), LY)

    def y_rows(k):
        return pl.ds(k, LX, stride=LY)

    def keep_x(kind, k, inverse, lower, ratio):
        inv_x[kind, x_rows(k), :] = inverse
        low_x[kind, x_rows(k), :] = lower
        rat_x[kind, x_rows(k), :] = ratio

    def keep_x_ends(kind, k, first, last):
        first_x[kind, x_rows(k), :] = first
        last_x[kind, x_rows(k), :] = last

    def keep_y(kind, k, inverse, lower, ratio):
        inv_y[kind, pl.ds(k * LX, LX), :] = inverse
        low_y[kind, pl.ds(k * LX, LX), :] = lower
        rat_y[kind, pl.ds(k * LX, LX), :] = ratio

    def keep_y_ends(kind, k, first, last):
        first_y[kind, y_rows(k), :] = first
        last_y[kind, y_rows(k), :] = last

    visc_in.wait()
    tiles = {}
    keep_factor(lambda k: vbuf[x_rows(k), :], LX, keep_x, keep_x_ends, tiles)
    for r in range(8):
        cxs[pl.ds(r, LY, stride=8), :] = tiles[r]

    for copy in flow_in:
        copy.wait()
    pl.semaphore_wait(barrier, len(known))
    greet(meet, column)

    def halo(n, src, dst, device):
        return pltpu.make_async_remote_copy(
            src_ref=src,
            dst_ref=dst,
            send_sem=halo_send.at[n],
            recv_sem=halo_recv.at[n],
            device_id=device,
            device_id_type=MESH,
        )

    x_up = halo(0, flat.at[:, cells(LX - 1), :], xh_low, up)
    x_down = halo(1, flat.at[:, cells(0), :], xh_high, down)
    y_up = halo(2, flow.at[:, :, LY - 1, :], yh_low, right)
    y_down = halo(3, flow.at[:, :, 0, :], yh_high, left)
    pl.when(has_up)(x_up.start)
    pl.when(has_down)(x_down.start)
    pl.when(has_right)(y_up.start)
    pl.when(has_left)(y_down.start)

    def send(src, there, dst, here, size, n, device):
        return pltpu.make_async_remote_copy(
            src_ref=src.at[pl.ds(pl.multiple_of(there * size, 8), size), :],
            dst_ref=dst.at[pl.ds(pl.multiple_of(here * size, 8), size), :],
            send_sem=send_sem.at[n],
            recv_sem=recv_sem.at[n],
            device_id=device,
            device_id_type=MESH,
        )

    def spread_x(src, dst, n):
        for peer in x_peers:
            send(src, peer, dst, gx, 8, n, (peer, other)).start()

    def spread_part(src, dst, n, own_row):
        for dx, dz in far_first(ring_x, ring_z):
            if (dx == 0) == own_row:
                peer = on_x(dx, dz)
                send(src, peer, dst, gx, 8, n, (peer, other)).start()

    def gather_y(src, dst, n):
        for chip in y_peers[:-1]:
            send(src, chip, dst, gy, piece, n, (gx, chip * cores + 1)).start()
        near = send(src, cy, dst, gy, piece, n, (gx, other))
        pl.when(cc == 0)(near.start)

        @pl.when(cc == 1)
        def _():
            dst[pl.ds(pl.multiple_of(gy * piece, 8), piece), :] = src[
                pl.ds(pl.multiple_of(cy * piece, 8), piece), :
            ]

    def spread_y(src, dst, n):
        for chip in y_peers[:-1]:
            for core in range(cores):
                peer = chip * cores + core
                send(src, peer, dst, cy, piece, n, (gx, peer)).start()
        send(src, other, dst, cy, piece, n, (gx, other)).start()
        dst[pl.ds(pl.multiple_of(cy * piece, 8), piece), :] = src[
            pl.ds(pl.multiple_of(gy * piece, 8), piece), :
        ]

    def take(ref, sem, n, rows):
        part = ref.at[pl.ds(0, rows), :]
        pltpu.make_async_copy(part, part, sem.at[n]).wait()

    def arrived(dst, n, rows):
        take(dst, recv_sem, n, rows)

    def departed(src, n, rows):
        take(src, send_sem, n, rows)

    spread_part(cxs, cxr, 0, True)
    all_x = 8 * PX
    to_core_1 = (PY - 1) * piece

    def source_row(k, sums):
        here = [flat[f, cells(k), :] for f in range(NF)]
        firsts, lasts = [], []
        for f in range(NF):
            across_x = flat[f, cells(k + 1), :] - flat[f, cells(k - 1), :]
            across_y = flat[f, cells(k, 1), :] - flat[f, cells(k, -1), :]
            across_z = pltpu.roll(here[f], NZ - 1, 1) - pltpu.roll(here[f], 1, 1)
            carried = here[0] * across_x + here[1] * across_y + here[2] * across_z
            source = here[f] - (0.5 * ADVECT) * carried
            if f == 2:
                source = source + BUOYANT * here[3]
            cur[f, x_rows(k), :] = source
            kind = KIND_OF[f]
            firsts.append(sums[f] + first_x[kind, x_rows(k), :] * source)
            lasts.append(sums[NF + f] + last_x[kind, x_rows(k), :] * source)
        return tuple(firsts + lasts)

    sums = (slab,) * (2 * NF)
    for k in range(LX):
        sums = source_row(k, sums)
    for r in range(8):
        xs[pl.ds(r, LY, stride=8), :] = sums[r]

    pl.semaphore_wait(meet, len(column))
    spread_part(cxs, cxr, 0, False)
    tiles = {}
    keep_factor(lambda k: vbuf[y_rows(k), :], LY, keep_y, keep_y_ends, tiles)
    for r in range(8):
        cys[pl.ds(r, LX, stride=8), :] = tiles[r]
    gather_y(cys, cyr, 1)

    half = 0.5 * ADVECT
    pl.when(has_left)(y_up.wait_recv)
    pl.when(has_right)(y_down.wait_recv)
    for at, around, sign in ((0, yh_low, half), (LY - 1, yh_high, -half)):
        speed = sign * flat[1, pl.ds(wide + Y0 + at, LX, stride=wide), :]
        for f in range(NF):
            kind = KIND_OF[f]
            change = speed * around[f]
            cur[f, y_rows(at), :] = cur[f, y_rows(at), :] + change
            for r, weight in ((f, first_x), (NF + f, last_x)):
                row = pl.ds(at * 8 + r, 1)
                total = jnp.sum(weight[kind, y_rows(at), :] * change, axis=0, keepdims=True)
                xs[row, :] = xs[row, :] + total
    pl.when(has_down)(x_up.wait_recv)
    pl.when(has_up)(x_down.wait_recv)
    for r, at, around, sign in ((0, 0, xh_low, half), (NF, LX - 1, xh_high, -half)):
        speed = sign * flat[0, cells(at), :]
        for f in range(NF):
            row = pl.ds(r + f, LY, stride=8)
            xs[row, :] = xs[row, :] + speed * around[f]
    spread_x(xs, xr, 2)

    def x_down_row(k, before):
        result = []
        for f in range(NF):
            kind = KIND_OF[f]
            value = inv_x[kind, x_rows(k), :] * cur[f, x_rows(k), :] + low_x[kind, x_rows(k), :] * before[f]
            inner[f, x_rows(k), :] = value
            result.append(value)
        return tuple(result)

    def x_up_row(step, after):
        k = LX - 3 - step
        result = []
        for f in range(NF):
            value = inner[f, x_rows(k), :] + rat_x[KIND_OF[f], x_rows(k), :] * after[f]
            inner[f, x_rows(k), :] = value
            result.append(value)
        return tuple(result)

    tail = lax.fori_loop(1, LX - 1, x_down_row, (slab,) * NF)
    lax.fori_loop(0, LX - 3, x_up_row, tail)

    arrived(cxr, 0, all_x)
    interface_factor(cxr, lambda b: 8 * b, PX, xi)
    arrived(xr, 2, all_x)
    interface_solve(xr, xb, lambda b: 8 * b, PX, xi)
    spread_x(xb, xg, 3)

    @pl.when(cc == 1)
    def _():
        arrived(cyr, 1, to_core_1)
        for t in range(piece // 8):
            base = lambda b, t=t: piece * b + 8 * t
            interface_factor(cyr, base, PY, [ref.at[t] for ref in yi])

    arrived(xg, 3, all_x)

    for f in range(NF):
        kind = KIND_OF[f]
        start, end = xg[pl.ds(f, LY, stride=8), :], xg[pl.ds(NF + f, LY, stride=8), :]

        def x_row(k, carry, f=f, kind=kind, start=start, end=end):
            rows = x_rows(k)
            value = inner[f, rows, :] + first_x[kind, rows, :] * start + last_x[kind, rows, :] * end
            cur[f, rows, :] = value
            for r, weight in ((f, first_y), (NF + f, last_y)):
                share = weight[kind, rows, :] * value
                total = share[0:8]
                for q in range(8, LY, 8):
                    total = total + share[q : q + 8]
                part[pl.ds(pl.multiple_of(k * 64, 8) + 8 * r, 8), :] = total
            return carry

        lax.fori_loop(0, LX, x_row, 0, unroll=4)
    for k in range(LX):
        total = part[pl.ds(64 * k, 8, stride=8), :]
        for q in range(1, 8):
            total = total + part[pl.ds(64 * k + q, 8, stride=8), :]
        ys[pl.ds(8 * k, 8), :] = total
    gather_y(ys, yr, 4)

    before = [edge] * NF
    for k in range(1, LY - 1):
        rows = pl.ds(k * LX, LX)
        for f in range(NF):
            kind = KIND_OF[f]
            before[f] = inv_y[kind, rows, :] * cur[f, y_rows(k), :] + low_y[kind, rows, :] * before[f]
            inner[f, rows, :] = before[f]
    after = before
    for f in range(NF):
        inner_y[f, y_rows(LY - 2), :] = after[f]
    for k in range(LY - 3, 0, -1):
        rows = pl.ds(k * LX, LX)
        for f in range(NF):
            after[f] = inner[f, rows, :] + rat_y[KIND_OF[f], rows, :] * after[f]
            inner_y[f, y_rows(k), :] = after[f]

    @pl.when(cc == 1)
    def _():
        arrived(yr, 4, to_core_1)
        for t in range(piece // 8):
            base = lambda b, t=t: piece * b + 8 * t
            interface_solve(yr, yb, base, PY, [ref.at[t] for ref in yi])
        spread_y(yb, yg, 5)

    pl.when(has_up)(x_up.wait_send)
    pl.when(has_down)(x_down.wait_send)
    pl.when(has_right)(y_up.wait_send)
    pl.when(has_left)(y_down.wait_send)
    departed(cxs, 0, all_x)
    departed(xs, 2, all_x)
    departed(xb, 3, all_x)

    @pl.when(cc == 0)
    def _():
        departed(cys, 1, ring_y * piece)
        departed(ys, 4, ring_y * piece)
        arrived(yg, 5, ring_y * piece)

    @pl.when(cc == 1)
    def _():
        if ring_y > 1:
            departed(cys, 1, (ring_y - 1) * piece)
            departed(ys, 4, (ring_y - 1) * piece)
            arrived(yg, 5, (ring_y - 1) * piece)
        departed(yb, 5, to_core_1)


CHUNK = 4


def assemble(inner, first, last, ends, out, done, sem):
    copies = []
    for k in range(LX):
        rows = pl.ds(k * LY, LY)
        for f in range(NF):
            kind = KIND_OF[f]
            done[f, rows, :] = (
                inner[f, rows, :]
                + first[kind, rows, :] * ends[pl.ds(8 * k + f, 1), :]
                + last[kind, rows, :] * ends[pl.ds(8 * k + NF + f, 1), :]
            )
        if k % CHUNK == CHUNK - 1:
            rows = pl.ds((k + 1 - CHUNK) * LY, CHUNK * LY)
            copies.append(
                pltpu.make_async_copy(done.at[:, rows, :], out.at[:, rows, :], sem.at[k // CHUNK])
            )
            copies[-1].start()
    for copy in copies:
        copy.wait()


def per_device(flow_state, viscosity):
    f32 = jnp.float32
    vmem = lambda *shape: pltpu.VMEM(shape, f32)
    rows = LX * LY
    in_vmem = pl.BlockSpec(memory_space=pltpu.VMEM)
    kept = pl.pallas_call(
        kernel,
        out_shape=[
            vmem(NF, rows, NZ),
            vmem(2, rows, NZ),
            vmem(2, rows, NZ),
            vmem(8 * LX, NZ),
        ],
        in_specs=[pl.BlockSpec(memory_space=pl.ANY)] * 2,
        out_specs=[in_vmem] * 4,
        scratch_shapes=[
            vmem(NF, (LX + 2) * (LY + 16), NZ),
            vmem(rows, NZ),
            vmem(NF, rows, NZ),
            vmem(NF, rows, NZ),
            vmem(LX * 64, NZ),
            *[vmem(2, rows, NZ)] * 8,
            *[vmem(PX + 1, 8, NZ)] * 3,
            *[vmem(8, PY + 1, 8, NZ)] * 3,
            *[vmem(8 * PX, NZ)] * 2,
            vmem(8 * LX, NZ),
            vmem(16 * LX, NZ),
            *[vmem(8 * PX, NZ)] * 4,
            vmem(8 * LX, NZ),
            *[vmem(16 * LX, NZ)] * 2,
            *[vmem(NF, LY, NZ)] * 2,
            *[vmem(NF, LX, NZ)] * 2,
            pltpu.SemaphoreType.DMA((1 + LX,)),
            pltpu.SemaphoreType.DMA((6,)),
            pltpu.SemaphoreType.DMA((6,)),
            pltpu.SemaphoreType.DMA((4,)),
            pltpu.SemaphoreType.DMA((4,)),
            pltpu.SemaphoreType.REGULAR,
        ],
        compiler_params=pltpu.CompilerParams(collective_id=0, has_side_effects=True),
    )(flow_state, viscosity.reshape(rows, NZ))
    result = pl.pallas_call(
        assemble,
        out_shape=jax.ShapeDtypeStruct((NF, rows, NZ), f32),
        in_specs=[in_vmem] * 4,
        out_specs=pl.BlockSpec(memory_space=pl.ANY),
        scratch_shapes=[vmem(NF, rows, NZ), pltpu.SemaphoreType.DMA((LX // CHUNK,))],
        compiler_params=pltpu.CompilerParams(vmem_limit_bytes=8 << 20),
    )(*kept)
    return result.reshape(NF, LX, LY, NZ)


def solution(mesh):
    return jax.shard_map(
        per_device,
        mesh=mesh,
        in_specs=(P(None, "gx", "gy", None), P("gx", "gy", None)),
        out_specs=P(None, "gx", "gy", None),
        check_vma=False,
    )
```

```python
import jax
import jax.numpy as jnp
from jax import lax
from jax.experimental import pallas as pl
from jax.experimental.pallas import tpu as pltpu
from jax.sharding import PartitionSpec as P

MESH = pl.DeviceIdType.MESH

ADVECT = 0.2
BUOYANT = 0.5
CONDUCT = 0.6
KINDS = (1.0, CONDUCT)
KIND_OF = (0, 0, 0, 1)

NF = 4
LX, LY, NZ = 16, 32, 128
PX, PY = 32, 8
Y0 = 8


def factor(faces, along):
    inverse, lower, ratio = {}, {}, {}
    one = jnp.ones_like(faces[1])
    running = one
    forward = {}
    for k in range(1, along - 1):
        centre = 1.0 + faces[k] + faces[k + 1]
        if k > 1:
            centre = centre - faces[k] * ratio[k - 1]
        inverse[k] = 1.0 / centre
        lower[k] = faces[k] * inverse[k]
        ratio[k] = faces[k + 1] * inverse[k]
        running = lower[k] * running
        forward[k] = running
    first, last = {along - 1: jnp.zeros_like(one)}, {along - 1: one}
    for k in range(along - 2, 0, -1):
        first[k] = forward[k] + ratio[k] * first[k + 1]
        last[k] = ratio[k] * last[k + 1]
    first[0], last[0] = one, jnp.zeros_like(one)
    return inverse, lower, ratio, first, last


def keep_factor(load, along, keep, keep_ends, tiles):
    cells = [load(k) for k in range(along)]
    middles = [None] + [cells[k - 1] + cells[k] for k in range(1, along)]
    tiles[0] = cells[0]
    tiles[1] = cells[-1]
    for kind, scale in enumerate(KINDS):
        faces = [None] + [(0.5 * scale) * m for m in middles[1:]]
        inverse, lower, ratio, first, last = factor(faces, along)
        for k in range(1, along - 1):
            keep(kind, k, inverse[k], lower[k], ratio[k])
        for k in range(along):
            keep_ends(kind, k, first[k], last[k])
        tiles[2 + kind] = 1.0 + faces[1] * (1.0 - first[1])
        tiles[4 + kind] = faces[1] * last[1]
        tiles[6 + kind] = 1.0 + faces[along - 1] * (1.0 - last[along - 2])


def rolled(value):
    return pltpu.roll(value, 4, 0)


def interface_factor(coef, base, blocks, refs):
    inv_ref, low_ref, rat_ref = refs
    sub = lax.broadcasted_iota(jnp.int32, (8, NZ), 0)
    down = sub < 4
    thermal = (sub == 3) | (sub == 7)

    def row(block, r):
        return jnp.broadcast_to(coef[pl.ds(base(block) + r, 1), :], (8, NZ))

    def by_kind(block, r):
        return jnp.where(thermal, row(block, r + 1), row(block, r))

    scale = jnp.where(thermal, CONDUCT, 1.0).astype(jnp.float32)
    half = blocks // 2
    sides = []
    for i in range(half + 1):
        if i == 0:
            value = jnp.where(down, row(0, 0), row(blocks - 1, 1))
        elif i == half:
            value = 0.5 * (row(i - 1, 1) + row(i, 0))
        else:
            value = 0.5 * jnp.where(
                down,
                row(i - 1, 1) + row(i, 0),
                row(blocks - 1 - i, 1) + row(blocks - i, 0),
            )
        sides.append(scale * value)
    ratio = None
    for i in range(half):
        j = blocks - 1 - i
        couple = jnp.where(down, by_kind(i, 4), by_kind(j, 4))
        even = jnp.where(down, by_kind(i, 2), by_kind(j, 6)) + sides[i]
        odd = jnp.where(down, by_kind(i, 6), by_kind(j, 2)) + sides[i + 1]
        for m, centre, before, after in (
            (2 * i, even, sides[i], couple),
            (2 * i + 1, odd, couple, sides[i + 1]),
        ):
            if m > 0:
                centre = centre - before * ratio
            inverse = 1.0 / centre
            ratio = after * inverse
            inv_ref[m] = inverse
            low_ref[m] = before * inverse
            rat_ref[m] = ratio
    inv_ref[blocks] = 1.0 / (1.0 - ratio * rolled(ratio))


def interface_solve(right, solved, base, blocks, refs):
    inv_ref, low_ref, rat_ref = refs
    down = lax.broadcasted_iota(jnp.int32, (8, NZ), 0) < 4
    half = blocks // 2
    forward = []
    for i in range(half):
        j = blocks - 1 - i
        mine, other = right[pl.ds(base(i), 8), :], right[pl.ds(base(j), 8), :]
        even = jnp.where(down, mine, other)
        odd = rolled(jnp.where(down, other, mine))
        for m, value in ((2 * i, even), (2 * i + 1, odd)):
            value = inv_ref[m] * value
            if m > 0:
                value = value + low_ref[m] * forward[-1]
            forward.append(value)
    tail = forward[-1]
    values = [None] * blocks
    values[-1] = (tail + rat_ref[blocks - 1] * rolled(tail)) * inv_ref[blocks]
    for m in range(blocks - 2, -1, -1):
        values[m] = forward[m] + rat_ref[m] * values[m + 1]
    for i in range(half):
        j = blocks - 1 - i
        even, odd = values[2 * i], rolled(values[2 * i + 1])
        solved[pl.ds(base(i), 8), :] = jnp.where(down, even, odd)
        solved[pl.ds(base(j), 8), :] = jnp.where(down, odd, even)


def far_first(size_a, size_b):
    hops = lambda d, size: min(d, size - d)
    offsets = [(a, b) for a in range(size_a) for b in range(size_b)]
    return sorted(offsets, key=lambda o: -hops(o[0], size_a) - hops(o[1], size_b))


def kernel(flow, visc, inner_y, first_y, last_y, yg, flat, vbuf, cur, inner, part, *rest):
    inv_x, low_x, rat_x, first_x, last_x = rest[0:5]
    inv_y, low_y, rat_y = rest[5:8]
    xi, yi = rest[8:11], rest[11:14]
    cxs, cxr, cys, cyr, xs, xr, xb, xg, ys, yr, yb = rest[14:25]
    xh_low, xh_high, yh_low, yh_high = rest[25:29]
    in_sem, send_sem, recv_sem, halo_send, halo_recv, meet = rest[29:]
    gx, gy = lax.axis_index("gx"), lax.axis_index("gy")

    barrier = pltpu.get_barrier_semaphore()
    ring_z, cores = 8, 2
    ring_x, ring_y = PX // ring_z, PY // cores
    cx, cz = lax.div(gx, ring_z), lax.rem(gx, ring_z)
    cy, cc = lax.div(gy, cores), lax.rem(gy, cores)
    other = cy * cores + 1 - cc
    piece = LX * 8 // ring_y

    def on_x(dx, dz):
        return lax.rem(cx + dx, ring_x) * ring_z + lax.rem(cz + dz, ring_z)

    x_peers = [on_x(dx, dz) for dx, dz in far_first(ring_x, ring_z)]
    y_peers = [lax.rem(cy + dy, ring_y) for dy, _ in far_first(ring_y, 1)]
    col_dx = [dx for dx, _ in far_first(ring_x, 1)[:-1]]
    column = [(on_x(dx, 0), gy) for dx, _ in far_first(ring_x, 1)[:-1]]
    up, down = (lax.rem(gx + 1, PX), gy), (lax.rem(gx + PX - 1, PX), gy)
    right, left = (gx, lax.rem(gy + 1, PY)), (gx, lax.rem(gy + PY - 1, PY))
    known = [(on_x(0, dz), other) for _, dz in far_first(1, ring_z)] + column + [up, down]
    known += [(gx, chip * cores + core) for chip in y_peers[:-1] for core in range(cores)]

    def greet(sem, devices):
        for device in devices:
            pl.semaphore_signal(sem, inc=1, device_id=device, device_id_type=MESH)

    greet(barrier, known)

    visc_in = pltpu.make_async_copy(visc, vbuf, in_sem.at[0])
    visc_in.start()
    wide = LY + 16

    def cells(k, shift=0):
        return pl.ds((k + 1) * wide + Y0 + shift, LY)

    flow_in = [
        pltpu.make_async_copy(flow.at[:, k], flat.at[:, cells(k), :], in_sem.at[1 + k])
        for k in range(LX)
    ]
    for copy in flow_in:
        copy.start()

    slab, edge = jnp.zeros((LY, NZ), jnp.float32), jnp.zeros((LX, NZ), jnp.float32)
    for f in range(NF):
        flat[f, cells(-1), :] = slab
        flat[f, cells(LX), :] = slab
        flat[f, pl.ds(wide + Y0 - 1, LX, stride=wide), :] = edge
        flat[f, pl.ds(wide + Y0 + LY, LX, stride=wide), :] = edge
        inner[f, pl.ds(0, LY), :] = slab
        inner[f, pl.ds((LX - 1) * LY, LY), :] = slab
        inner_y[f, pl.ds(0, LX, stride=LY), :] = edge
        inner_y[f, pl.ds(LY - 1, LX, stride=LY), :] = edge

    has_up, has_down = gx < PX - 1, gx > 0
    has_right, has_left = gy < PY - 1, gy > 0

    @pl.when(gx == 0)
    def _():
        xh_low[...] = jnp.zeros_like(xh_low)

    @pl.when(gx == PX - 1)
    def _():
        xh_high[...] = jnp.zeros_like(xh_high)

    @pl.when(gy == 0)
    def _():
        yh_low[...] = jnp.zeros_like(yh_low)

    @pl.when(gy == PY - 1)
    def _():
        yh_high[...] = jnp.zeros_like(yh_high)

    def x_rows(k):
        return pl.ds(pl.multiple_of(k * LY, 8), LY)

    def y_rows(k):
        return pl.ds(k, LX, stride=LY)

    def keep_x(kind, k, inverse, lower, ratio):
        inv_x[kind, x_rows(k), :] = inverse
        low_x[kind, x_rows(k), :] = lower
        rat_x[kind, x_rows(k), :] = ratio

    def keep_x_ends(kind, k, first, last):
        first_x[kind, x_rows(k), :] = first
        last_x[kind, x_rows(k), :] = last

    def keep_y(kind, k, inverse, lower, ratio):
        inv_y[kind, pl.ds(k * LX, LX), :] = inverse
        low_y[kind, pl.ds(k * LX, LX), :] = lower
        rat_y[kind, pl.ds(k * LX, LX), :] = ratio

    def keep_y_ends(kind, k, first, last):
        first_y[kind, y_rows(k), :] = first
        last_y[kind, y_rows(k), :] = last

    visc_in.wait()
    tiles = {}
    keep_factor(lambda k: vbuf[x_rows(k), :], LX, keep_x, keep_x_ends, tiles)
    for r in range(8):
        cxs[pl.ds(r, LY, stride=8), :] = tiles[r]

    for copy in flow_in:
        copy.wait()
    pl.semaphore_wait(barrier, len(known))
    for n, device in enumerate(column):
        pl.semaphore_signal(meet.at[n], inc=1, device_id=device, device_id_type=MESH)

    def halo(n, src, dst, device):
        return pltpu.make_async_remote_copy(
            src_ref=src,
            dst_ref=dst,
            send_sem=halo_send.at[n],
            recv_sem=halo_recv.at[n],
            device_id=device,
            device_id_type=MESH,
        )

    x_up = halo(0, flat.at[:, cells(LX - 1), :], xh_low, up)
    x_down = halo(1, flat.at[:, cells(0), :], xh_high, down)
    y_up = halo(2, flow.at[:, :, LY - 1, :], yh_low, right)
    y_down = halo(3, flow.at[:, :, 0, :], yh_high, left)
    pl.when(has_up)(x_up.start)
    pl.when(has_down)(x_down.start)
    pl.when(has_right)(y_up.start)
    pl.when(has_left)(y_down.start)

    def send(src, there, dst, here, size, n, device):
        return pltpu.make_async_remote_copy(
            src_ref=src.at[pl.ds(pl.multiple_of(there * size, 8), size), :],
            dst_ref=dst.at[pl.ds(pl.multiple_of(here * size, 8), size), :],
            send_sem=send_sem.at[n],
            recv_sem=recv_sem.at[n],
            device_id=device,
            device_id_type=MESH,
        )

    def spread_x(src, dst, n):
        for peer in x_peers:
            send(src, peer, dst, gx, 8, n, (peer, other)).start()

    def spread_part(src, dst, n, own_row):
        for dx, dz in far_first(ring_x, ring_z):
            if (dx == 0) == own_row:
                peer = on_x(dx, dz)
                send(src, peer, dst, gx, 8, n, (peer, other)).start()

    def gather_y(src, dst, n):
        for chip in y_peers[:-1]:
            send(src, chip, dst, gy, piece, n, (gx, chip * cores + 1)).start()
        near = send(src, cy, dst, gy, piece, n, (gx, other))
        pl.when(cc == 0)(near.start)

        @pl.when(cc == 1)
        def _():
            dst[pl.ds(pl.multiple_of(gy * piece, 8), piece), :] = src[
                pl.ds(pl.multiple_of(cy * piece, 8), piece), :
            ]

    def spread_y(src, dst, n):
        for chip in y_peers[:-1]:
            for core in range(cores):
                peer = chip * cores + core
                send(src, peer, dst, cy, piece, n, (gx, peer)).start()
        send(src, other, dst, cy, piece, n, (gx, other)).start()
        dst[pl.ds(pl.multiple_of(cy * piece, 8), piece), :] = src[
            pl.ds(pl.multiple_of(gy * piece, 8), piece), :
        ]

    def take(ref, sem, n, rows):
        part = ref.at[pl.ds(0, rows), :]
        pltpu.make_async_copy(part, part, sem.at[n]).wait()

    def arrived(dst, n, rows):
        take(dst, recv_sem, n, rows)

    def departed(src, n, rows):
        take(src, send_sem, n, rows)

    spread_part(cxs, cxr, 0, True)
    all_x = 8 * PX
    to_core_1 = (PY - 1) * piece

    def source_row(k, sums):
        here = [flat[f, cells(k), :] for f in range(NF)]
        firsts, lasts = [], []
        for f in range(NF):
            across_x = flat[f, cells(k + 1), :] - flat[f, cells(k - 1), :]
            across_y = flat[f, cells(k, 1), :] - flat[f, cells(k, -1), :]
            across_z = pltpu.roll(here[f], NZ - 1, 1) - pltpu.roll(here[f], 1, 1)
            carried = here[0] * across_x + here[1] * across_y + here[2] * across_z
            source = here[f] - (0.5 * ADVECT) * carried
            if f == 2:
                source = source + BUOYANT * here[3]
            cur[f, x_rows(k), :] = source
            kind = KIND_OF[f]
            firsts.append(sums[f] + first_x[kind, x_rows(k), :] * source)
            lasts.append(sums[NF + f] + last_x[kind, x_rows(k), :] * source)
        return tuple(firsts + lasts)

    sums = (slab,) * (2 * NF)
    for k in range(LX):
        sums = source_row(k, sums)
    for r in range(8):
        xs[pl.ds(r, LY, stride=8), :] = sums[r]

    for n in range(1, len(column) + 1):
        came = len(column) - n
        dx = (ring_x - col_dx[came]) % ring_x
        pl.semaphore_wait(meet.at[came], 1)
        for _, dz in far_first(1, ring_z):
            peer = on_x(dx, dz)
            send(cxs, peer, cxr, gx, 8, 0, (peer, other)).start()
    half = 0.5 * ADVECT
    pl.when(has_left)(y_up.wait_recv)
    pl.when(has_right)(y_down.wait_recv)
    for at, around, sign in ((0, yh_low, half), (LY - 1, yh_high, -half)):
        speed = sign * flat[1, pl.ds(wide + Y0 + at, LX, stride=wide), :]
        for f in range(NF):
            kind = KIND_OF[f]
            change = speed * around[f]
            cur[f, y_rows(at), :] = cur[f, y_rows(at), :] + change
            for r, weight in ((f, first_x), (NF + f, last_x)):
                row = pl.ds(at * 8 + r, 1)
                total = jnp.sum(weight[kind, y_rows(at), :] * change, axis=0, keepdims=True)
                xs[row, :] = xs[row, :] + total
    pl.when(has_down)(x_up.wait_recv)
    pl.when(has_up)(x_down.wait_recv)
    for r, at, around, sign in ((0, 0, xh_low, half), (NF, LX - 1, xh_high, -half)):
        speed = sign * flat[0, cells(at), :]
        for f in range(NF):
            row = pl.ds(r + f, LY, stride=8)
            xs[row, :] = xs[row, :] + speed * around[f]
    spread_x(xs, xr, 2)

    def x_down_row(k, before):
        result = []
        for f in range(NF):
            kind = KIND_OF[f]
            value = inv_x[kind, x_rows(k), :] * cur[f, x_rows(k), :] + low_x[kind, x_rows(k), :] * before[f]
            inner[f, x_rows(k), :] = value
            result.append(value)
        return tuple(result)

    def x_up_row(step, after):
        k = LX - 3 - step
        result = []
        for f in range(NF):
            value = inner[f, x_rows(k), :] + rat_x[KIND_OF[f], x_rows(k), :] * after[f]
            inner[f, x_rows(k), :] = value
            result.append(value)
        return tuple(result)

    tail = lax.fori_loop(1, LX - 1, x_down_row, (slab,) * NF)
    lax.fori_loop(0, LX - 3, x_up_row, tail)

    tiles = {}
    keep_factor(lambda k: vbuf[y_rows(k), :], LY, keep_y, keep_y_ends, tiles)
    for r in range(8):
        cys[pl.ds(r, LX, stride=8), :] = tiles[r]
    gather_y(cys, cyr, 1)

    arrived(cxr, 0, all_x)
    interface_factor(cxr, lambda b: 8 * b, PX, xi)
    arrived(xr, 2, all_x)
    interface_solve(xr, xb, lambda b: 8 * b, PX, xi)
    spread_x(xb, xg, 3)

    @pl.when(cc == 1)
    def _():
        arrived(cyr, 1, to_core_1)
        for t in range(piece // 8):
            base = lambda b, t=t: piece * b + 8 * t
            interface_factor(cyr, base, PY, [ref.at[t] for ref in yi])

    arrived(xg, 3, all_x)

    for f in range(NF):
        kind = KIND_OF[f]
        start, end = xg[pl.ds(f, LY, stride=8), :], xg[pl.ds(NF + f, LY, stride=8), :]

        def x_row(k, carry, f=f, kind=kind, start=start, end=end):
            rows = x_rows(k)
            value = inner[f, rows, :] + first_x[kind, rows, :] * start + last_x[kind, rows, :] * end
            cur[f, rows, :] = value
            for r, weight in ((f, first_y), (NF + f, last_y)):
                share = weight[kind, rows, :] * value
                total = share[0:8]
                for q in range(8, LY, 8):
                    total = total + share[q : q + 8]
                part[pl.ds(pl.multiple_of(k * 64, 8) + 8 * r, 8), :] = total
            return carry

        lax.fori_loop(0, LX, x_row, 0, unroll=4)
    for k in range(LX):
        total = part[pl.ds(64 * k, 8, stride=8), :]
        for q in range(1, 8):
            total = total + part[pl.ds(64 * k + q, 8, stride=8), :]
        ys[pl.ds(8 * k, 8), :] = total
    gather_y(ys, yr, 4)

    before = [edge] * NF
    for k in range(1, LY - 1):
        rows = pl.ds(k * LX, LX)
        for f in range(NF):
            kind = KIND_OF[f]
            before[f] = inv_y[kind, rows, :] * cur[f, y_rows(k), :] + low_y[kind, rows, :] * before[f]
            inner[f, rows, :] = before[f]
    after = before
    for f in range(NF):
        inner_y[f, y_rows(LY - 2), :] = after[f]
    for k in range(LY - 3, 0, -1):
        rows = pl.ds(k * LX, LX)
        for f in range(NF):
            after[f] = inner[f, rows, :] + rat_y[KIND_OF[f], rows, :] * after[f]
            inner_y[f, y_rows(k), :] = after[f]

    @pl.when(cc == 1)
    def _():
        arrived(yr, 4, to_core_1)
        for t in range(piece // 8):
            base = lambda b, t=t: piece * b + 8 * t
            interface_solve(yr, yb, base, PY, [ref.at[t] for ref in yi])
        spread_y(yb, yg, 5)

    pl.when(has_up)(x_up.wait_send)
    pl.when(has_down)(x_down.wait_send)
    pl.when(has_right)(y_up.wait_send)
    pl.when(has_left)(y_down.wait_send)
    departed(cxs, 0, all_x)
    departed(xs, 2, all_x)
    departed(xb, 3, all_x)

    @pl.when(cc == 0)
    def _():
        departed(cys, 1, ring_y * piece)
        departed(ys, 4, ring_y * piece)
        arrived(yg, 5, ring_y * piece)

    @pl.when(cc == 1)
    def _():
        if ring_y > 1:
            departed(cys, 1, (ring_y - 1) * piece)
            departed(ys, 4, (ring_y - 1) * piece)
            arrived(yg, 5, (ring_y - 1) * piece)
        departed(yb, 5, to_core_1)


CHUNK = 4


def assemble(inner, first, last, ends, out, done, sem):
    copies = []
    for k in range(LX):
        rows = pl.ds(k * LY, LY)
        for f in range(NF):
            kind = KIND_OF[f]
            done[f, rows, :] = (
                inner[f, rows, :]
                + first[kind, rows, :] * ends[pl.ds(8 * k + f, 1), :]
                + last[kind, rows, :] * ends[pl.ds(8 * k + NF + f, 1), :]
            )
        if k % CHUNK == CHUNK - 1:
            rows = pl.ds((k + 1 - CHUNK) * LY, CHUNK * LY)
            copies.append(
                pltpu.make_async_copy(done.at[:, rows, :], out.at[:, rows, :], sem.at[k // CHUNK])
            )
            copies[-1].start()
    for copy in copies:
        copy.wait()


def per_device(flow_state, viscosity):
    f32 = jnp.float32
    vmem = lambda *shape: pltpu.VMEM(shape, f32)
    rows = LX * LY
    in_vmem = pl.BlockSpec(memory_space=pltpu.VMEM)
    kept = pl.pallas_call(
        kernel,
        out_shape=[
            vmem(NF, rows, NZ),
            vmem(2, rows, NZ),
            vmem(2, rows, NZ),
            vmem(8 * LX, NZ),
        ],
        in_specs=[pl.BlockSpec(memory_space=pl.ANY)] * 2,
        out_specs=[in_vmem] * 4,
        scratch_shapes=[
            vmem(NF, (LX + 2) * (LY + 16), NZ),
            vmem(rows, NZ),
            vmem(NF, rows, NZ),
            vmem(NF, rows, NZ),
            vmem(LX * 64, NZ),
            *[vmem(2, rows, NZ)] * 8,
            *[vmem(PX + 1, 8, NZ)] * 3,
            *[vmem(8, PY + 1, 8, NZ)] * 3,
            *[vmem(8 * PX, NZ)] * 2,
            vmem(8 * LX, NZ),
            vmem(16 * LX, NZ),
            *[vmem(8 * PX, NZ)] * 4,
            vmem(8 * LX, NZ),
            *[vmem(16 * LX, NZ)] * 2,
            *[vmem(NF, LY, NZ)] * 2,
            *[vmem(NF, LX, NZ)] * 2,
            pltpu.SemaphoreType.DMA((1 + LX,)),
            pltpu.SemaphoreType.DMA((6,)),
            pltpu.SemaphoreType.DMA((6,)),
            pltpu.SemaphoreType.DMA((4,)),
            pltpu.SemaphoreType.DMA((4,)),
            pltpu.SemaphoreType.REGULAR((3,)),
        ],
        compiler_params=pltpu.CompilerParams(collective_id=0, has_side_effects=True),
    )(flow_state, viscosity.reshape(rows, NZ))
    result = pl.pallas_call(
        assemble,
        out_shape=jax.ShapeDtypeStruct((NF, rows, NZ), f32),
        in_specs=[in_vmem] * 4,
        out_specs=pl.BlockSpec(memory_space=pl.ANY),
        scratch_shapes=[vmem(NF, rows, NZ), pltpu.SemaphoreType.DMA((LX // CHUNK,))],
        compiler_params=pltpu.CompilerParams(vmem_limit_bytes=8 << 20),
    )(*kept)
    return result.reshape(NF, LX, LY, NZ)


def solution(mesh):
    return jax.shard_map(
        per_device,
        mesh=mesh,
        in_specs=(P(None, "gx", "gy", None), P("gx", "gy", None)),
        out_specs=P(None, "gx", "gy", None),
        check_vma=False,
    )
```
